256 devices in a mesh: src: 16 (over z, core), tgt: 16 (over y, x).
Axes of the slice: x: 4, y: 4, z: 8, core: 2. Of those that a mesh axis runs over, the one named last changes fastest.
Arguments:
- source: float32 [32, 16384], P(None, ('src', 'tgt')), may hold values from -2 to 2
- target: float32 [32, 26624], P(None, ('tgt', 'src')), may hold values from -2 to 2
- target_pot: float32 [26624], P(('tgt', 'src')), may hold values from -1 to 8
- source_logw: float32 [16384], P(('src', 'tgt')), may hold values from -14 to -9
- target_logw: float32 [26624], P(('tgt', 'src')), may hold values from -14 to -9
Outputs:
- f_new: float32 [16384], P(('src', 'tgt'))
- g_new: float32 [26624], P(('tgt', 'src'))
- projection: float32 [32, 16384], P(None, ('src', 'tgt'))
The draws below stay inside these ranges and needn't reach their ends.
All inputs are finite; a program needn't handle non-finite values.
Results may differ from the reference program's by a relative error of at most 0.0003.
Values sent between devices are 32-bit elements; how exact they have to be, the bound alone decides.
A program may use at most 64 MiB of HBM per device.

```python
import math
import jax
import jax.numpy as jnp
from jax import lax

D = 32
NS = 16384
NT = 26624


def shared_cells(key):
    key_source = jax.random.fold_in(key, 101)
    key_target = jax.random.fold_in(key, 102)
    source = jnp.clip(0.2 * jax.random.normal(key_source, (D, NS), jnp.float32), -1.2, 1.2)
    target = jnp.clip(0.2 * jax.random.normal(key_target, (D, NT), jnp.float32), -1.2, 1.2)
    return (source, target)


def draw_source(key, part):
    return shared_cells(key)[0]


def draw_target(key, part):
    return shared_cells(key)[1]


def draw_target_pot(key, part):
    key_pot = jax.random.fold_in(key, 201)
    potential = jnp.clip(0.3 * jax.random.normal(key_pot, (NT,), jnp.float32), -1.0, 1.0)
    return potential


def block_scale(stream_key, shape, shards, low, largest):
    factor_of = 1.0
    for position, blocks in shards:
        draws = jax.random.uniform(jax.random.fold_in(jax.random.fold_in(stream_key, 6), position), (blocks,), jnp.float32, low / len(shards), largest / len(shards))
        factor_of = factor_of * jnp.repeat(jnp.exp(draws), shape[position] // blocks).reshape((-1,) + (1,) * (len(shape) - 1 - position))
    return factor_of


def setup_inputs(seed: int = 0) -> dict:
    streams_of = jax.random.split(jax.random.key(seed), 6)
    return {
        "source": draw_source(jax.random.fold_in(streams_of[5], 71), 0),
        "target": draw_target(jax.random.fold_in(streams_of[5], 71), 0),
        "target_pot": draw_target_pot(jax.random.fold_in(streams_of[5], 71), 0),
        "source_logw": jnp.clip(-14.0 + 5.0 * jax.random.uniform(streams_of[3], (NS,), jnp.float32) ** block_scale(streams_of[3], (NS,), ((0, 256),), -0.2, 0.2), -14.0, -9.0),
        "target_logw": jnp.clip(-14.0 + 5.0 * jax.random.uniform(streams_of[4], (NT,), jnp.float32) ** block_scale(streams_of[4], (NT,), ((0, 256),), -0.2, 0.2), -14.0, -9.0),
    }


EPSILON = 0.05
HIGHEST = lax.Precision.HIGHEST


def log_sums(row_cells, col_cells, col_pot, col_logw, weighted):
    feat_dim, row_count = row_cells.shape
    row_block = math.gcd(row_count, 1024)
    col_sq = jnp.sum(col_cells * col_cells, 0)
    blocks = row_cells.reshape(feat_dim, row_count // row_block, row_block).transpose(1, 0, 2)

    def one_block(cells_block):
        cross_term = lax.dot_general(cells_block, col_cells, (((0,), (0,)), ((), ())), precision=HIGHEST, preferred_element_type=jnp.float32)
        cost_tile = jnp.sum(cells_block * cells_block, 0)[:, None] + col_sq[None, :] - 2.0 * cross_term
        scores = (col_pot[None, :] - cost_tile) / EPSILON + col_logw[None, :]
        row_top = jnp.max(scores, 1)
        kernel = jnp.exp(scores - row_top[:, None])
        totals = jnp.sum(kernel, 1)
        if weighted:
            moments = lax.dot_general(col_cells, kernel, (((1,), (1,)), ((), ())), precision=HIGHEST, preferred_element_type=jnp.float32)
            return row_top, totals, moments
        return row_top, totals

    result = lax.map(one_block, blocks)
    row_top = result[0].reshape(row_count)
    totals = result[1].reshape(row_count)
    if weighted:
        moments = result[2].transpose(1, 0, 2).reshape(feat_dim, row_count)
        return row_top, totals, moments
    return row_top, totals


def reference(source, target, target_pot, source_logw, target_logw):
    row_top, row_totals = log_sums(source, target, target_pot, target_logw, False)
    f_new = -EPSILON * (row_top + jnp.log(row_totals))
    col_top, col_totals = log_sums(target, source, f_new, source_logw, False)
    g_new = -EPSILON * (col_top + jnp.log(col_totals))
    proj_top, proj_totals, moments = log_sums(source, target, g_new, target_logw, True)
    projection = moments / proj_totals[None, :]
    return f_new, g_new, projection
```

```python
import math

import jax
import jax.numpy as jnp
from jax import lax
from jax.experimental import pallas as pl
from jax.experimental.pallas import tpu as pltpu
from jax.sharding import PartitionSpec as P

EPSILON = 0.05
LOG2E = 1.0 / math.log(2.0)
SCALE = LOG2E / EPSILON
F32 = jnp.float32
BF16 = jnp.bfloat16
MESH = pl.DeviceIdType.MESH
GROUP = 16
ROWS = 1024
COLS = 1664
OWN_ROWS = 64
OWN_COLS = 104
DIM = 32


def dot(a, b):
    return lax.dot_general(a, b, (((1,), (0,)), ((), ())), preferred_element_type=F32)


def split3(x):
    one = x.astype(BF16).astype(F32)
    rest = x - one
    two = rest.astype(BF16).astype(F32)
    return one, two, rest - two


def lane_iota(rows):
    return lax.broadcasted_iota(jnp.int32, (rows, 128), 1)


def sub_iota(rows):
    return lax.broadcasted_iota(jnp.int32, (rows, 128), 0)


def bias_rows(bias):
    one, two, three = split3(bias)
    sub = sub_iota(8)
    return jnp.where(sub == 0, one, jnp.where(sub == 1, two, jnp.where(sub == 2, three, 0.0)))


def combine(parts):
    top = parts[0]
    for part in parts[1:]:
        top = jnp.maximum(top, part)
    total = jnp.exp2(parts[0] - top)
    for part in parts[1:]:
        total = total + jnp.exp2(part - top)
    return top + jnp.log(total) * LOG2E


def column_pieces(block):
    start, pieces = block * 128, []
    while start < block * 128 + 128:
        shard, offset = divmod(start, OWN_COLS)
        stop = min((shard + 1) * OWN_COLS, block * 128 + 128)
        pieces.append((shard, offset, start - block * 128, stop - block * 128))
        start = stop
    return pieces


def kernel(
    src_ref, tgt_ref, pot_ref, slw_ref, tlw_ref,
    f_ref, g_ref, p_ref,
    pad, smsg, tmsg, srecv, trecv,
    xr, yr, xt, yt, tl,
    slw, tlw, lsend, lrecv, gsend, grecv, msend, mrecv, lall, gall,
    s_send, s_recv, t_send, t_recv, l_send, l_recv, g_send, g_recv, m_send, m_recv,
):
    me_t = lax.axis_index("tgt")
    me_s = lax.axis_index("src")

    def peer_t(k):
        return lax.rem(me_t + k, GROUP)

    def peer_s(k):
        return lax.rem(me_s + k, GROUP)

    barrier = pltpu.get_barrier_semaphore()

    def greet(k, carry):
        pl.semaphore_signal(barrier, inc=1, device_id={"tgt": peer_t(k)}, device_id_type=MESH)
        pl.semaphore_signal(barrier, inc=1, device_id={"src": peer_s(k)}, device_id_type=MESH)
        return carry

    lax.fori_loop(1, GROUP, greet, 0)

    pad[...] = jnp.zeros_like(pad)
    pad[0:DIM, 0:OWN_ROWS] = src_ref[...]
    pad[DIM : DIM + 1, 0:OWN_ROWS] = slw_ref[...] * LOG2E
    own = pad[...]
    src_sq = jnp.sum(own[0:DIM] * own[0:DIM], 0, keepdims=True)
    low = lane_iota(16) < 64
    smsg[0:16, :] = jnp.where(low, own[0:16], pltpu.roll(own[16:32], 64, 1))
    smsg[16:24, :] = own[32:40]
    tmsg[...] = jnp.zeros_like(tmsg)
    tmsg[0:DIM, 0:OWN_COLS] = tgt_ref[...]
    own_t = tmsg[0:DIM, :]
    tgt_sq = jnp.sum(own_t * own_t, 0, keepdims=True)
    tmsg[DIM : DIM + 1, 0:OWN_COLS] = (
        SCALE * (pot_ref[...] - tgt_sq[:, 0:OWN_COLS]) + LOG2E * tlw_ref[...]
    )
    tmsg[DIM + 1 : DIM + 2, 0:OWN_COLS] = LOG2E * tlw_ref[...]

    pl.semaphore_wait(barrier, 2 * (GROUP - 1))

    def over_t(src_at, dst, send, recv, k):
        return pltpu.make_async_remote_copy(
            src_ref=src_at, dst_ref=dst.at[me_t], send_sem=send.at[k], recv_sem=recv.at[me_t],
            device_id={"tgt": peer_t(k)}, device_id_type=MESH,
        )

    def over_s(src_at, dst, send, recv, k):
        return pltpu.make_async_remote_copy(
            src_ref=src_at, dst_ref=dst.at[me_s], send_sem=send.at[k], recv_sem=recv.at[me_s],
            device_id={"src": peer_s(k)}, device_id_type=MESH,
        )

    def wait_arrivals(dst, recv, peer):
        def one(k, carry):
            other = peer(k)
            pltpu.make_async_copy(dst.at[other], dst.at[other], recv.at[other]).wait()
            return carry

        lax.fori_loop(1, GROUP, one, 0)

    def loop(step):
        def one(k, carry):
            step(k)
            return carry

        lax.fori_loop(1, GROUP, one, 0)

    def send_cells(k):
        over_s(tmsg, trecv, t_send, t_recv, k).start()
        over_t(smsg, srecv, s_send, s_recv, k).start()

    loop(send_cells)
    srecv[me_t] = smsg[...]
    trecv[me_s] = tmsg[...]

    wait_arrivals(srecv, s_recv, peer_t)
    ones16 = jnp.where(sub_iota(16) < 3, 1.0, 0.0).astype(BF16)
    zeros48 = jnp.zeros((48, 128), BF16)
    zeros56 = jnp.zeros((56, 128), F32)
    for p in range(8):
        a, b = srecv[2 * p], srecv[2 * p + 1]
        first = jnp.where(low, a[0:16], pltpu.roll(b[0:16], 64, 1))
        second = jnp.where(low, pltpu.roll(a[0:16], 64, 1), b[0:16])
        x = jnp.concatenate([first, second], 0) * (2.0 * SCALE)
        x1, x2, x3 = split3(x)
        at = slice(128 * p, 128 * p + 128)
        slw[p : p + 1, :] = jnp.where(low[0:1], a[16:17], pltpu.roll(b[16:24], 64, 1)[0:1])
        top = jnp.concatenate([x1, x1, x2, x2], 0)
        end = jnp.concatenate([x1, x3], 0)
        xr[0:128, at] = top.astype(BF16)
        xr[128:192, at] = end.astype(BF16)
        xr[192:208, at] = ones16
        xr[208:256, at] = zeros48
        xt[at, 0:128] = jnp.transpose(top).astype(BF16)

    wait_arrivals(trecv, t_recv, peer_s)
    for q in range(13):
        at = slice(128 * q, 128 * q + 128)
        lane = lane_iota(40)
        block = None
        for shard, offset, start, stop in column_pieces(q):
            piece = trecv[shard]
            shift = (start - offset) % 128
            if shift:
                piece = pltpu.roll(piece, shift, 1)
            block = piece if block is None else jnp.where(lane >= start, piece, block)
        y1, y2, y3 = split3(block[0:DIM])
        tlw[q : q + 1, :] = block[DIM + 1 : DIM + 2]
        top = jnp.concatenate([y1, y2, y1, y2], 0)
        end = jnp.concatenate([y3, y1], 0)
        yr[0:128, at] = top.astype(BF16)
        yr[128:192, at] = end.astype(BF16)
        yr[192:208, at] = ones16
        yr[208:256, at] = zeros48
        tl[0:64, at] = yr[0:64, at]
        tl[64:96, at] = yr[128:160, at]
        tl[96:112, at] = jnp.ones((16, 128), BF16)
        yt[at, 0:128] = jnp.transpose(top).astype(BF16)
        tail = jnp.concatenate([end, bias_rows(block[DIM : DIM + 1]), zeros56], 0)
        yt[at, 128:256] = jnp.transpose(tail).astype(BF16)

    for n in range(4):
        scores = dot(yt[...], xr[:, 256 * n : 256 * n + 256])
        top = jnp.max(scores, 0, keepdims=True)
        part = top + jnp.log(jnp.sum(jnp.exp2(scores - top), 0, keepdims=True)) * LOG2E
        lsend[2 * n : 2 * n + 1, :] = part[:, 0:128]
        lsend[2 * n + 1 : 2 * n + 2, :] = part[:, 128:256]
    loop(lambda k: over_t(lsend, lrecv, l_send, l_recv, k).start())
    lrecv[me_t] = lsend[...]
    wait_arrivals(lrecv, l_recv, peer_t)
    row_lse = combine([lrecv[k] for k in range(GROUP)])
    lall[...] = row_lse
    for p in range(8):
        at = slice(128 * p, 128 * p + 128)
        bias = slw[p : p + 1, :] - row_lse[p : p + 1, :]
        tail = jnp.concatenate([xr[128:192, at].astype(F32), bias_rows(bias), zeros56], 0)
        xt[at, 128:256] = jnp.transpose(tail).astype(BF16)

    for n in range(7):
        width = 256 if n < 6 else 128
        scores = dot(xt[...], yr[:, 256 * n : 256 * n + width])
        top = jnp.max(scores, 0, keepdims=True)
        part = top + jnp.log(jnp.sum(jnp.exp2(scores - top), 0, keepdims=True)) * LOG2E
        for h in range(width // 128):
            gsend[2 * n + h : 2 * n + h + 1, :] = part[:, 128 * h : 128 * h + 128]
    gsend[13:16, :] = jnp.zeros((3, 128), F32)
    loop(lambda k: over_s(gsend, grecv, g_send, g_recv, k).start())
    grecv[me_s] = gsend[...]

    row = lall[pl.ds(me_t // 2, 1), :]
    row = jnp.where(lax.rem(me_t, 2) == 1, pltpu.roll(row, 64, 1), row)
    f_ref[...] = (src_sq - (EPSILON / LOG2E) * row)[:, 0:OWN_ROWS]

    wait_arrivals(grecv, g_recv, peer_s)
    col_lse = combine([grecv[k] for k in range(GROUP)])
    gall[...] = col_lse
    for q in range(13):
        at = slice(128 * q, 128 * q + 128)
        bias = tlw[q : q + 1, :] - col_lse[q : q + 1, :]
        tail = jnp.concatenate([yr[128:192, at].astype(F32), bias_rows(bias), zeros56], 0)
        yt[at, 128:256] = jnp.transpose(tail).astype(BF16)

    low40 = lane_iota(40) < 64
    for n in range(4):
        scores = dot(yt[...], xr[:, 256 * n : 256 * n + 256])
        top = jnp.max(scores, 0, keepdims=True)
        weights = jnp.exp2(scores - top)
        high = weights.astype(BF16)
        rest = (weights - high.astype(F32)).astype(BF16)
        moments = dot(tl[...], high) + dot(tl[...], rest)
        message = jnp.concatenate(
            [
                moments[0:32] + moments[32:64] + moments[64:96],
                jnp.where(lax.broadcasted_iota(jnp.int32, (8, 256), 0) == 0, moments[96:104], top),
            ],
            0,
        )
        for h in range(2):
            half = message[:, 128 * h : 128 * h + 128]
            msend[4 * n + 2 * h] = half
            msend[4 * n + 2 * h + 1] = pltpu.roll(half, 64, 1)
    loop(lambda k: over_t(msend.at[peer_t(k)], mrecv, m_send, m_recv, k).start())
    mrecv[me_t] = msend[me_t]

    start = me_s * OWN_COLS
    line, offset = start // 128, lax.rem(start, 128)
    here = pltpu.roll(gall[pl.ds(line, 1), :], 128 - offset, 1)
    after = pltpu.roll(gall[pl.ds(line + 1, 1), :], 128 - offset, 1)
    col = jnp.where(lane_iota(1) < 128 - offset, here, after)
    g_ref[...] = (tgt_sq - (EPSILON / LOG2E) * col)[:, 0:OWN_COLS]

    wait_arrivals(mrecv, m_recv, peer_t)
    parts = [mrecv[k] for k in range(GROUP)]
    top = parts[0][33:34]
    for part in parts[1:]:
        top = jnp.maximum(top, part[33:34])
    total = jnp.zeros((40, 128), F32)
    for part in parts:
        total = total + part * jnp.exp2(part[33:34] - top)
    p_ref[...] = (total[0:32] / total[32:33])[:, 0:OWN_ROWS]

    def finish(k):
        over_s(tmsg, trecv, t_send, t_recv, k).wait_send()
        over_t(smsg, srecv, s_send, s_recv, k).wait_send()
        over_t(lsend, lrecv, l_send, l_recv, k).wait_send()
        over_s(gsend, grecv, g_send, g_recv, k).wait_send()
        over_t(msend.at[peer_t(k)], mrecv, m_send, m_recv, k).wait_send()

    loop(finish)


def body(source, target, target_pot, source_logw, target_logw):
    vmem = pl.BlockSpec(memory_space=pltpu.VMEM)
    f_new, g_new, projection = pl.pallas_call(
        kernel,
        out_shape=(
            jax.ShapeDtypeStruct((1, OWN_ROWS), F32),
            jax.ShapeDtypeStruct((1, OWN_COLS), F32),
            jax.ShapeDtypeStruct((DIM, OWN_ROWS), F32),
        ),
        in_specs=[vmem] * 5,
        out_specs=(vmem,) * 3,
        scratch_shapes=[
            pltpu.VMEM((40, 128), F32),
            pltpu.VMEM((24, 128), F32),
            pltpu.VMEM((40, 128), F32),
            pltpu.VMEM((GROUP, 24, 128), F32),
            pltpu.VMEM((GROUP, 40, 128), F32),
            pltpu.VMEM((256, ROWS), BF16),
            pltpu.VMEM((256, COLS), BF16),
            pltpu.VMEM((ROWS, 256), BF16),
            pltpu.VMEM((COLS, 256), BF16),
            pltpu.VMEM((112, COLS), BF16),
            pltpu.VMEM((8, 128), F32),
            pltpu.VMEM((16, 128), F32),
            pltpu.VMEM((8, 128), F32),
            pltpu.VMEM((GROUP, 8, 128), F32),
            pltpu.VMEM((16, 128), F32),
            pltpu.VMEM((GROUP, 16, 128), F32),
            pltpu.VMEM((GROUP, 40, 128), F32),
            pltpu.VMEM((GROUP, 40, 128), F32),
            pltpu.VMEM((8, 128), F32),
            pltpu.VMEM((16, 128), F32),
        ]
        + [pltpu.SemaphoreType.DMA((GROUP,))] * 10,
        compiler_params=pltpu.CompilerParams(
            collective_id=0, has_side_effects=True, vmem_limit_bytes=60 * 1024 * 1024
        ),
    )(
        source,
        target,
        target_pot.reshape(1, OWN_COLS),
        source_logw.reshape(1, OWN_ROWS),
        target_logw.reshape(1, OWN_COLS),
    )
    return f_new.reshape(OWN_ROWS), g_new.reshape(OWN_COLS), projection


def solution(mesh):
    return jax.shard_map(
        body,
        mesh=mesh,
        in_specs=(
            P(None, ("src", "tgt")),
            P(None, ("tgt", "src")),
            P(("tgt", "src")),
            P(("src", "tgt")),
            P(("tgt", "src")),
        ),
        out_specs=(P(("src", "tgt")), P(("tgt", "src")), P(None, ("src", "tgt"))),
        check_vma=False,
    )
```

```python
import math

import jax
import jax.numpy as jnp
from jax import lax
from jax.experimental import pallas as pl
from jax.experimental.pallas import tpu as pltpu
from jax.sharding import PartitionSpec as P

EPSILON = 0.05
LOG2E = 1.0 / math.log(2.0)
SCALE = LOG2E / EPSILON
F32 = jnp.float32
BF16 = jnp.bfloat16
MESH = pl.DeviceIdType.MESH
GROUP = 16
ROWS = 1024
COLS = 1664
OWN_ROWS = 64
OWN_COLS = 104
DIM = 32
SRC_LINES = 17
TGT_LINES = 34
HALVES = ((0, 1024), (1024, 640))


def ring(d, n):
    return min(d, n - d)


TGT_PEERS = sorted(
    [(y, x) for y in range(4) for x in range(4) if y or x],
    key=lambda o: -(ring(o[0], 4) + ring(o[1], 4)),
)
SRC_PEERS = sorted(
    [(z, c) for z in range(8) for c in range(2) if z or c],
    key=lambda o: (-ring(o[0], 8), o[1]),
)
Z_PEERS = (4, 3, 5, 2, 6, 1, 7)
Z_ARRIVALS = (1, 7, 2, 6, 3, 5, 4)


def dot(a, b):
    return lax.dot_general(a, b, (((1,), (0,)), ((), ())), preferred_element_type=F32)


def split3(x):
    one = x.astype(BF16).astype(F32)
    rest = x - one
    two = rest.astype(BF16).astype(F32)
    return one, two, rest - two


def lane_iota(rows):
    return lax.broadcasted_iota(jnp.int32, (rows, 128), 1)


def sub_iota(rows):
    return lax.broadcasted_iota(jnp.int32, (rows, 128), 0)


def bias_rows(bias):
    one, two, three = split3(bias)
    sub = sub_iota(8)
    return jnp.where(sub == 0, one, jnp.where(sub == 1, two, jnp.where(sub == 2, three, 0.0)))


def combine(parts):
    top = parts[0]
    for part in parts[1:]:
        top = jnp.maximum(top, part)
    total = jnp.exp2(parts[0] - top)
    for part in parts[1:]:
        total = total + jnp.exp2(part - top)
    return top + jnp.log(total) * LOG2E


def column_pieces(block):
    start, pieces = block * 128, []
    while start < block * 128 + 128:
        shard, offset = divmod(start, OWN_COLS)
        stop = min((shard + 1) * OWN_COLS, block * 128 + 128)
        pieces.append((shard, offset, start - block * 128, stop - block * 128))
        start = stop
    return pieces


def lse(scores):
    top = jnp.max(scores, 0, keepdims=True)
    return top + jnp.log(jnp.sum(jnp.exp2(scores - top), 0, keepdims=True)) * LOG2E


def kernel(
    src_hbm, tgt_hbm, pot_hbm, slw_hbm, tlw_hbm,
    f_ref, g_ref, p_ref,
    src_v, tgt_v, pot_v, slw_v, tlw_v,
    pad, smsg, tmsg, srecv, trecv,
    xr, yr, xt, yt, tl,
    slw, tlw, lpart, lsend, lrecv, gsend, grecv, moms, tops, msend, mrecv, lall, gall,
    in_sem, s_send, s_recv, t_send, t_recv, l_send, l_recv, g_send, g_recv, m_send, m_recv,
):
    me_t = lax.axis_index("tgt")
    me_s = lax.axis_index("src")
    me_y, me_x = me_t // 4, lax.rem(me_t, 4)
    me_z, me_c = me_s // 2, lax.rem(me_s, 2)

    def at_t(offset):
        return lax.rem(me_y + offset[0], 4) * 4 + lax.rem(me_x + offset[1], 4)

    def at_s(offset):
        return lax.rem(me_z + offset[0], 8) * 2 + lax.rem(me_c + offset[1], 2)

    barrier = pltpu.get_barrier_semaphore()
    for offset in TGT_PEERS:
        pl.semaphore_signal(barrier, inc=1, device_id={"tgt": at_t(offset)}, device_id_type=MESH)
    for offset in SRC_PEERS:
        pl.semaphore_signal(barrier, inc=1, device_id={"src": at_s(offset)}, device_id_type=MESH)

    inputs = [
        pltpu.make_async_copy(a, b, in_sem.at[n])
        for n, (a, b) in enumerate(
            ((src_hbm, src_v), (slw_hbm, slw_v), (tgt_hbm, tgt_v), (pot_hbm, pot_v), (tlw_hbm, tlw_v))
        )
    ]
    for copy in inputs:
        copy.start()
    pad[...] = jnp.zeros_like(pad)
    tmsg[...] = jnp.zeros_like(tmsg)
    low = lane_iota(16) < 64
    for copy in inputs:
        copy.wait()

    pad[0:DIM, 0:OWN_ROWS] = src_v[...]
    pad[DIM : DIM + 1, 0:OWN_ROWS] = slw_v[...] * LOG2E
    own = pad[...]
    src_sq = jnp.sum(own[0:DIM] * own[0:DIM], 0, keepdims=True)
    smsg[0:16, :] = jnp.where(low, own[0:16], pltpu.roll(own[16:32], 64, 1))
    smsg[16:24, :] = own[32:40]
    tmsg[0:DIM, 0:OWN_COLS] = tgt_v[...]
    own_t = tmsg[0:DIM, :]
    tgt_sq = jnp.sum(own_t * own_t, 0, keepdims=True)
    tmsg[DIM : DIM + 1, 0:OWN_COLS] = (
        SCALE * (pot_v[...] - tgt_sq[:, 0:OWN_COLS]) + LOG2E * tlw_v[...]
    )
    tmsg[DIM + 1 : DIM + 2, 0:OWN_COLS] = LOG2E * tlw_v[...]

    pl.semaphore_wait(barrier, 2 * (GROUP - 1))
    sent = []

    def to_t(offset, src, dst, send, recv):
        copy = pltpu.make_async_remote_copy(
            src_ref=src, dst_ref=dst, send_sem=send, recv_sem=recv.at[me_t],
            device_id={"tgt": at_t(offset)}, device_id_type=MESH,
        )
        copy.start()
        sent.append(copy)

    def to_s(offset, slot, src, dst, send, recv):
        copy = pltpu.make_async_remote_copy(
            src_ref=src, dst_ref=dst, send_sem=send, recv_sem=recv.at[slot],
            device_id={"src": at_s(offset)}, device_id_type=MESH,
        )
        copy.start()
        sent.append(copy)

    def arrive(dst, sem):
        pltpu.make_async_copy(dst, dst, sem).wait()

    tgt_own = tmsg.at[0:TGT_LINES]
    for n, z in enumerate(Z_PEERS):
        to_s((z, 0), me_s, tgt_own, trecv.at[me_s, 0:TGT_LINES], t_send.at[n], t_recv)
    to_s((0, 1), me_s, tgt_own, trecv.at[me_s, 0:TGT_LINES], t_send.at[7], t_recv)
    src_own = smsg.at[0:SRC_LINES]
    for n, offset in enumerate(TGT_PEERS):
        to_t(offset, src_own, srecv.at[me_t, 0:SRC_LINES], s_send.at[n], s_recv)
    srecv[me_t] = smsg[...]
    trecv[me_s] = tmsg[...]
    ones16 = jnp.where(sub_iota(16) < 3, 1.0, 0.0).astype(BF16)
    zeros48 = jnp.zeros((48, 128), BF16)
    zeros56 = jnp.zeros((56, 128), F32)

    for offset in reversed(TGT_PEERS):
        slot = at_t(offset)
        arrive(srecv.at[slot, 0:SRC_LINES], s_recv.at[slot])
    for p in range(8):
        a, b = srecv[2 * p], srecv[2 * p + 1]
        first = jnp.where(low, a[0:16], pltpu.roll(b[0:16], 64, 1))
        second = jnp.where(low, pltpu.roll(a[0:16], 64, 1), b[0:16])
        x1, x2, x3 = split3(jnp.concatenate([first, second], 0) * (2.0 * SCALE))
        at = slice(128 * p, 128 * p + 128)
        slw[p : p + 1, :] = jnp.where(low[0:1], a[16:17], pltpu.roll(b[16:24], 64, 1)[0:1])
        xr[0:128, at] = jnp.concatenate([x1, x1, x2, x2], 0).astype(BF16)
        xr[128:192, at] = jnp.concatenate([x1, x3], 0).astype(BF16)
        xr[192:208, at] = ones16
        xr[208:256, at] = zeros48

    def take(n, z):
        pair = lax.rem(me_z + z, 8)
        tops_t, tails_t = [], []
        for c in range(2):
            block = trecv[2 * pair + c]
            y1, y2, y3 = split3(block[0:DIM])
            tops_t.append(jnp.transpose(jnp.concatenate([y1, y2, y1, y2], 0))[0:OWN_COLS])
            tail = jnp.concatenate([y3, y1, bias_rows(block[DIM : DIM + 1]), zeros56], 0)
            tails_t.append(jnp.transpose(tail)[0:OWN_COLS])
        at = pl.ds(pl.multiple_of(pair * (2 * OWN_COLS), 16), 2 * OWN_COLS)
        yt[at, 0:128] = jnp.concatenate(tops_t, 0).astype(BF16)
        yt[at, 128:256] = jnp.concatenate(tails_t, 0).astype(BF16)
        part = lse(dot(yt[at, :], xr[...]))
        for p in range(8):
            lpart[n, p : p + 1, :] = part[:, 128 * p : 128 * p + 128]

    partner = lax.rem(me_c + 1, 2)
    arrive(trecv.at[me_z * 2 + partner, 0:TGT_LINES], t_recv.at[me_z * 2 + partner])
    for n in range(8):
        if n < 7:
            pair = lax.rem(me_z + Z_ARRIVALS[n], 8)
            slot = pair * 2 + me_c
            here = trecv.at[slot, 0:TGT_LINES]
            arrive(here, t_recv.at[slot])
            to_s((0, 1), slot, here, here, t_send.at[8 + n], t_recv)
        take(n, 0 if n == 0 else Z_ARRIVALS[n - 1])
        if n < 7:
            slot = pair * 2 + partner
            arrive(trecv.at[slot, 0:TGT_LINES], t_recv.at[slot])
    lsend[...] = combine([lpart[n] for n in range(8)])
    for n, offset in enumerate(TGT_PEERS):
        to_t(offset, lsend, lrecv.at[me_t], l_send.at[n], l_recv)
    lrecv[me_t] = lsend[...]

    for p in range(8):
        at = slice(128 * p, 128 * p + 128)
        xt[at, 0:128] = jnp.transpose(xr[0:128, at].astype(F32)).astype(BF16)
    for q in range(13):
        at = slice(128 * q, 128 * q + 128)
        lane = lane_iota(40)
        block = None
        for shard, offset, start, stop in column_pieces(q):
            piece = trecv[shard]
            shift = (start - offset) % 128
            if shift:
                piece = pltpu.roll(piece, shift, 1)
            block = piece if block is None else jnp.where(lane >= start, piece, block)
        y1, y2, y3 = split3(block[0:DIM])
        tlw[q : q + 1, :] = block[DIM + 1 : DIM + 2]
        yr[0:128, at] = jnp.concatenate([y1, y2, y1, y2], 0).astype(BF16)
        yr[128:192, at] = jnp.concatenate([y3, y1], 0).astype(BF16)
        yr[192:208, at] = ones16
        yr[208:256, at] = zeros48
        tl[0:32, at] = y1.astype(BF16)
        tl[32:48, at] = jnp.ones((16, 128), BF16)
        tl[48:80, at] = y2.astype(BF16)

    for offset in reversed(TGT_PEERS):
        slot = at_t(offset)
        arrive(lrecv.at[slot], l_recv.at[slot])
    row_lse = combine([lrecv[k] for k in range(GROUP)])
    lall[...] = row_lse
    for p in range(8):
        at = slice(128 * p, 128 * p + 128)
        bias = slw[p : p + 1, :] - row_lse[p : p + 1, :]
        tail = jnp.concatenate([xr[128:192, at].astype(F32), bias_rows(bias), zeros56], 0)
        xt[at, 128:256] = jnp.transpose(tail).astype(BF16)

    for half, (base, count) in enumerate(HALVES):
        for start in range(0, count, 256):
            width = min(256, count - start)
            part = lse(dot(xt[...], yr[:, base + start : base + start + width]))
            for h in range(width // 128):
                line = start // 128 + h
                gsend[half, line : line + 1, :] = part[:, 128 * h : 128 * h + 128]
        lines = count // 128
        for n, offset in enumerate(SRC_PEERS):
            to_s(offset, half * GROUP + me_s, gsend.at[half, 0:lines], grecv.at[half, me_s, 0:lines],
                 g_send.at[half * GROUP + n], g_recv)
    for half in range(2):
        grecv[half, me_s] = gsend[half]

    row = lall[pl.ds(me_y * 2 + me_x // 2, 1), :]
    row = jnp.where(lax.rem(me_t, 2) == 1, pltpu.roll(row, 64, 1), row)
    f_ref[...] = (src_sq - (EPSILON / LOG2E) * row)[:, 0:OWN_ROWS]

    for half, (base, count) in enumerate(HALVES):
        lines = count // 128
        for offset in reversed(SRC_PEERS):
            slot = at_s(offset)
            arrive(grecv.at[half, slot, 0:lines], g_recv.at[half * GROUP + slot])
        if half == 1:
            pass
        col_lse = combine([grecv[half, k] for k in range(GROUP)])
        gall[8 * half : 8 * half + 8, :] = col_lse
        for line in range(lines):
            at = slice(base + 128 * line, base + 128 * line + 128)
            q = base // 128 + line
            bias = tlw[q : q + 1, :] - col_lse[line : line + 1, :]
            tail = jnp.concatenate([yr[128:192, at].astype(F32), bias_rows(bias), zeros56], 0)
            yt[at, 128:256] = jnp.transpose(tail).astype(BF16)
        span = slice(base, base + count)
        for order in ((0, 1, 2, 3), (2, 1, 3, 0))[half]:
            tile = lax.rem(me_y + order, 4)
            columns = pl.ds(pl.multiple_of(tile * 256, 256), 256)
            scores = dot(yt[span, :], xr[:, columns])
            top = jnp.max(scores, 0, keepdims=True)
            weights = jnp.exp2(scores - top)
            high = weights.astype(BF16)
            rest = (weights - high.astype(F32)).astype(BF16)
            main = dot(tl[0:80, span], high)
            moments = jnp.concatenate(
                [main[0:32] + main[48:80], main[32:40]], 0
            ) + dot(tl[0:48, span], rest)[0:40]
            if half == 0:
                moms[order] = moments
                tops[order] = jnp.broadcast_to(top, (8, 256))
                continue
            before = tops[order]
            both = jnp.maximum(before, top)
            fix_a, fix_b = jnp.exp2(before - both), jnp.exp2(top - both)
            moments = moms[order] * fix_a[0:1] + moments * fix_b[0:1]
            for u in range(4):
                lanes = slice(128 * (u // 2), 128 * (u // 2) + 128)
                one, two = moments[0:16, lanes], moments[16:32, lanes]
                three, four = moments[32:40, lanes], both[:, lanes]
                if u % 2 == 0:
                    two, four = pltpu.roll(two, 64, 1), pltpu.roll(four, 64, 1)
                else:
                    one, three = pltpu.roll(one, 64, 1), pltpu.roll(three, 64, 1)
                msend[tile * 4 + u, 0:16, :] = jnp.where(low, one, two)
                msend[tile * 4 + u, 16:24, :] = jnp.where(low[0:8], three, four)
            for x in range(0 if order else 1, 4):
                slot = tile * 4 + lax.rem(me_x + x, 4)
                to_t((order, x), msend.at[slot, 0:SRC_LINES], mrecv.at[me_t, 0:SRC_LINES],
                     m_send.at[order * 4 + x], m_recv)
    mrecv[me_t] = msend[me_t]

    start = me_s * OWN_COLS
    line, offset = start // 128, lax.rem(start, 128)
    here = pltpu.roll(gall[pl.ds(line, 1), :], 128 - offset, 1)
    after = pltpu.roll(gall[pl.ds(line + 1, 1), :], 128 - offset, 1)
    col = jnp.where(lane_iota(1) < 128 - offset, here, after)
    g_ref[...] = (tgt_sq - (EPSILON / LOG2E) * col)[:, 0:OWN_COLS]

    for offset in reversed(TGT_PEERS):
        slot = at_t(offset)
        arrive(mrecv.at[slot, 0:SRC_LINES], m_recv.at[slot])
    top = mrecv[0, 16:17, :]
    for k in range(1, GROUP):
        top = jnp.maximum(top, mrecv[k, 16:17, :])
    acc, norm = jnp.zeros((16, 128), F32), jnp.zeros((1, 128), F32)
    low1 = low[0:1]
    for k in range(GROUP):
        last = mrecv[k, 16:17, :]
        fix = jnp.exp2(last - top)
        fix = jnp.where(low1, pltpu.roll(fix, 64, 1), fix)
        acc = acc + mrecv[k, 0:16, :] * fix
        norm = norm + last * fix
    ratio = acc / jnp.where(low1, norm, pltpu.roll(norm, 64, 1))
    p_ref[0:16, :] = ratio[:, 0:OWN_ROWS]
    p_ref[16:32, :] = pltpu.roll(ratio, 64, 1)[:, 0:OWN_ROWS]
    for copy in sent:
        copy.wait_send()


def body(source, target, target_pot, source_logw, target_logw):
    vmem = pl.BlockSpec(memory_space=pltpu.VMEM)
    f_new, g_new, projection = pl.pallas_call(
        kernel,
        out_shape=(
            jax.ShapeDtypeStruct((1, OWN_ROWS), F32),
            jax.ShapeDtypeStruct((1, OWN_COLS), F32),
            jax.ShapeDtypeStruct((DIM, OWN_ROWS), F32),
        ),
        in_specs=[pl.BlockSpec(memory_space=pl.ANY)] * 5,
        out_specs=(vmem,) * 3,
        scratch_shapes=[
            pltpu.VMEM((DIM, OWN_ROWS), F32),
            pltpu.VMEM((DIM, OWN_COLS), F32),
            pltpu.VMEM((1, OWN_COLS), F32),
            pltpu.VMEM((1, OWN_ROWS), F32),
            pltpu.VMEM((1, OWN_COLS), F32),
            pltpu.VMEM((40, 128), F32),
            pltpu.VMEM((24, 128), F32),
            pltpu.VMEM((40, 128), F32),
            pltpu.VMEM((GROUP, 24, 128), F32),
            pltpu.VMEM((GROUP, 40, 128), F32),
            pltpu.VMEM((256, ROWS), BF16),
            pltpu.VMEM((256, COLS), BF16),
            pltpu.VMEM((ROWS, 256), BF16),
            pltpu.VMEM((COLS, 256), BF16),
            pltpu.VMEM((80, COLS), BF16),
            pltpu.VMEM((8, 128), F32),
            pltpu.VMEM((16, 128), F32),
            pltpu.VMEM((8, 8, 128), F32),
            pltpu.VMEM((8, 128), F32),
            pltpu.VMEM((GROUP, 8, 128), F32),
            pltpu.VMEM((2, 8, 128), F32),
            pltpu.VMEM((2, GROUP, 8, 128), F32),
            pltpu.VMEM((4, 40, 256), F32),
            pltpu.VMEM((4, 8, 256), F32),
            pltpu.VMEM((GROUP, 24, 128), F32),
            pltpu.VMEM((GROUP, 24, 128), F32),
            pltpu.VMEM((8, 128), F32),
            pltpu.VMEM((16, 128), F32),
            pltpu.SemaphoreType.DMA((5,)),
        ]
        + [pltpu.SemaphoreType.DMA((GROUP,))] * 6
        + [pltpu.SemaphoreType.DMA((2 * GROUP,))] * 2
        + [pltpu.SemaphoreType.DMA((GROUP,))] * 2,
        compiler_params=pltpu.CompilerParams(
            collective_id=0, has_side_effects=True, vmem_limit_bytes=60 * 1024 * 1024
        ),
    )(
        source,
        target,
        target_pot.reshape(1, OWN_COLS),
        source_logw.reshape(1, OWN_ROWS),
        target_logw.reshape(1, OWN_COLS),
    )
    return f_new.reshape(OWN_ROWS), g_new.reshape(OWN_COLS), projection


def solution(mesh):
    return jax.shard_map(
        body,
        mesh=mesh,
        in_specs=(
            P(None, ("src", "tgt")),
            P(None, ("tgt", "src")),
            P(("tgt", "src")),
            P(("src", "tgt")),
            P(("tgt", "src")),
        ),
        out_specs=(P(("src", "tgt")), P(("tgt", "src")), P(None, ("src", "tgt"))),
        check_vma=False,
    )
```

```python
import math

import jax
import jax.numpy as jnp
from jax import lax
from jax.experimental import pallas as pl
from jax.experimental.pallas import tpu as pltpu
from jax.sharding import PartitionSpec as P

EPSILON = 0.05
LOG2E = 1.0 / math.log(2.0)
SCALE = LOG2E / EPSILON
F32 = jnp.float32
BF16 = jnp.bfloat16
MESH = pl.DeviceIdType.MESH
GROUP = 16
ROWS = 1024
COLS = 1664
OWN_ROWS = 64
OWN_COLS = 104
DIM = 32
SRC_LINES = 17
TGT_LINES = 34
HALVES = ((0, 640), (640, 1024))


def ring(d, n):
    return min(d, n - d)


TGT_PEERS = sorted(
    [(y, x) for y in range(4) for x in range(4) if y or x],
    key=lambda o: -(ring(o[0], 4) + ring(o[1], 4)),
)
Z_PEERS = (4, 3, 5, 2, 6, 1, 7)
Z_NEAR = (1, 7, 2, 6)
Z_FAR = (3, 5, 4)


def dot(a, b):
    return lax.dot_general(a, b, (((1,), (0,)), ((), ())), preferred_element_type=F32)


def split3(x):
    one = x.astype(BF16).astype(F32)
    rest = x - one
    two = rest.astype(BF16).astype(F32)
    return one, two, rest - two


def lane_iota(rows):
    return lax.broadcasted_iota(jnp.int32, (rows, 128), 1)


def sub_iota(rows):
    return lax.broadcasted_iota(jnp.int32, (rows, 128), 0)


def bias_rows(bias):
    one, two, three = split3(bias)
    sub = sub_iota(8)
    return jnp.where(sub == 0, one, jnp.where(sub == 1, two, jnp.where(sub == 2, three, 0.0)))


def combine(parts):
    top = parts[0]
    for part in parts[1:]:
        top = jnp.maximum(top, part)
    total = jnp.exp2(parts[0] - top)
    for part in parts[1:]:
        total = total + jnp.exp2(part - top)
    return top + jnp.log(total) * LOG2E


def column_pieces(block):
    start, pieces = block * 128, []
    while start < block * 128 + 128:
        shard, offset = divmod(start, OWN_COLS)
        stop = min((shard + 1) * OWN_COLS, block * 128 + 128)
        pieces.append((shard, offset, start - block * 128, stop - block * 128))
        start = stop
    return pieces


def lse(scores):
    top = jnp.max(scores, 0, keepdims=True)
    return top + jnp.log(jnp.sum(jnp.exp2(scores - top), 0, keepdims=True)) * LOG2E


def kernel(
    src_hbm, tgt_hbm, pot_hbm, slw_hbm, tlw_hbm,
    f_ref, g_ref, p_ref,
    src_v, tgt_v, pot_v, slw_v, tlw_v,
    pad, smsg, tmsg, srecv, trecv,
    xr, yr, xt, yt, tl, ya, held, peak, scr,
    slw, tlw, lpart, lsend, lrecv, csend, crecv, gsend, grecv, moms, tops, msend, mrecv, lall, gall,
    in_sem, s_send, s_recv, t_send, t_recv, l_send, l_recv, g_send, g_recv, m_send, m_recv, c_send, c_recv,
):
    me_t = lax.axis_index("tgt")
    me_s = lax.axis_index("src")
    me_y, me_x = me_t // 4, lax.rem(me_t, 4)
    me_z, me_c = me_s // 2, lax.rem(me_s, 2)

    def at_t(offset):
        return lax.rem(me_y + offset[0], 4) * 4 + lax.rem(me_x + offset[1], 4)

    def at_s(offset):
        return lax.rem(me_z + offset[0], 8) * 2 + lax.rem(me_c + offset[1], 2)

    barrier = pltpu.get_barrier_semaphore()
    for offset in TGT_PEERS:
        pl.semaphore_signal(barrier, inc=1, device_id={"tgt": at_t(offset)}, device_id_type=MESH)
    for offset in [(z, 0) for z in Z_PEERS] + [(0, 1)]:
        pl.semaphore_signal(barrier, inc=1, device_id={"src": at_s(offset)}, device_id_type=MESH)

    inputs = [
        pltpu.make_async_copy(a, b, in_sem.at[n])
        for n, (a, b) in enumerate(
            ((src_hbm, src_v), (slw_hbm, slw_v), (tgt_hbm, tgt_v), (pot_hbm, pot_v), (tlw_hbm, tlw_v))
        )
    ]
    for copy in inputs:
        copy.start()
    pad[...] = jnp.zeros_like(pad)
    tmsg[...] = jnp.zeros_like(tmsg)
    low = lane_iota(16) < 64
    for copy in inputs:
        copy.wait()

    pad[0:DIM, 0:OWN_ROWS] = src_v[...]
    pad[DIM : DIM + 1, 0:OWN_ROWS] = slw_v[...] * LOG2E
    own = pad[...]
    src_sq = jnp.sum(own[0:DIM] * own[0:DIM], 0, keepdims=True)
    smsg[0:16, :] = jnp.where(low, own[0:16], pltpu.roll(own[16:32], 64, 1))
    smsg[16:24, :] = own[32:40]
    tmsg[0:DIM, 0:OWN_COLS] = tgt_v[...]
    own_t = tmsg[0:DIM, :]
    tgt_sq = jnp.sum(own_t * own_t, 0, keepdims=True)
    tmsg[DIM : DIM + 1, 0:OWN_COLS] = (
        SCALE * (pot_v[...] - tgt_sq[:, 0:OWN_COLS]) + LOG2E * tlw_v[...]
    )
    tmsg[DIM + 1 : DIM + 2, 0:OWN_COLS] = LOG2E * tlw_v[...]

    pl.semaphore_wait(barrier, len(TGT_PEERS) + len(Z_PEERS) + 1)
    sent = []

    def to_t(offset, src, dst, send, recv):
        copy = pltpu.make_async_remote_copy(
            src_ref=src, dst_ref=dst, send_sem=send, recv_sem=recv.at[me_t],
            device_id={"tgt": at_t(offset)}, device_id_type=MESH,
        )
        copy.start()
        sent.append(copy)

    def to_s(offset, slot, src, dst, send, recv):
        copy = pltpu.make_async_remote_copy(
            src_ref=src, dst_ref=dst, send_sem=send, recv_sem=recv.at[slot],
            device_id={"src": at_s(offset)}, device_id_type=MESH,
        )
        copy.start()
        sent.append(copy)

    def arrive(dst, sem):
        pltpu.make_async_copy(dst, dst, sem).wait()

    tgt_own = tmsg.at[0:TGT_LINES]
    for n, z in enumerate(Z_PEERS):
        to_s((z, 0), me_s, tgt_own, trecv.at[me_s, 0:TGT_LINES], t_send.at[n], t_recv)
    to_s((0, 1), me_s, tgt_own, trecv.at[me_s, 0:TGT_LINES], t_send.at[7], t_recv)
    src_own = smsg.at[0:SRC_LINES]
    for n, offset in enumerate(TGT_PEERS):
        to_t(offset, src_own, srecv.at[me_t, 0:SRC_LINES], s_send.at[n], s_recv)
    srecv[me_t] = smsg[...]
    trecv[me_s] = tmsg[...]
    ones16 = jnp.where(sub_iota(16) < 3, 1.0, 0.0).astype(BF16)
    zeros48 = jnp.zeros((48, 128), BF16)
    zeros56 = jnp.zeros((56, 128), F32)

    partner = lax.rem(me_c + 1, 2)

    def cells(slot):
        return trecv.at[slot, 0:TGT_LINES]

    def forward(n, z):
        slot = lax.rem(me_z + z, 8) * 2 + me_c
        arrive(cells(slot), t_recv.at[slot])
        to_s((0, 1), slot, cells(slot), cells(slot), t_send.at[8 + n], t_recv)

    def operand(n, slots):
        tops_t, tails_t = [], []
        for slot in slots:
            block = trecv[slot]
            y1, y2, y3 = split3(block[0:DIM])
            tops_t.append(jnp.transpose(jnp.concatenate([y1, y2, y1, y2], 0))[0:OWN_COLS])
            tail = jnp.concatenate([y3, y1, bias_rows(block[DIM : DIM + 1]), zeros56], 0)
            tails_t.append(jnp.transpose(tail)[0:OWN_COLS])
        ya[n, :, 0:128] = jnp.concatenate(tops_t, 0).astype(BF16)
        ya[n, :, 128:256] = jnp.concatenate(tails_t, 0).astype(BF16)

    def mine(z):
        return lax.rem(me_z + z, 8) * 2 + me_c

    def other(z):
        return lax.rem(me_z + z, 8) * 2 + partner

    def first(n):
        scores = dot(ya[n], xr[...])
        held[n % 2] = scores
        peak[n % 2] = jnp.max(scores, 0, keepdims=True)

    def second(n):
        top = peak[n % 2]
        part = top + jnp.log(jnp.sum(jnp.exp2(held[n % 2] - top), 0, keepdims=True)) * LOG2E
        for p in range(8):
            lpart[n, p : p + 1, :] = part[:, 128 * p : 128 * p + 128]

    arrive(cells(other(0)), t_recv.at[other(0)])
    operand(0, (me_s, other(0)))
    for n, z in enumerate(Z_NEAR):
        forward(n, z)
    operand(1, (mine(1), mine(7)))
    operand(2, (mine(2), mine(6)))

    for offset in reversed(TGT_PEERS):
        slot = at_t(offset)
        arrive(srecv.at[slot, 0:SRC_LINES], s_recv.at[slot])
    for p in range(8):
        a, b = srecv[2 * p], srecv[2 * p + 1]
        one = jnp.where(low, a[0:16], pltpu.roll(b[0:16], 64, 1))
        two = jnp.where(low, pltpu.roll(a[0:16], 64, 1), b[0:16])
        x1, x2, x3 = split3(jnp.concatenate([one, two], 0) * (2.0 * SCALE))
        at = slice(128 * p, 128 * p + 128)
        slw[p : p + 1, :] = jnp.where(low[0:1], a[16:17], pltpu.roll(b[16:24], 64, 1)[0:1])
        xr[0:128, at] = jnp.concatenate([x1, x1, x2, x2], 0).astype(BF16)
        xr[128:192, at] = jnp.concatenate([x1, x3], 0).astype(BF16)
        xr[192:208, at] = ones16
        xr[208:256, at] = zeros48
    for n, z in enumerate(Z_FAR):
        forward(4 + n, z)
    operand(3, (mine(3), mine(5)))
    first(0)
    first(1)
    second(0)
    first(2)
    second(1)
    first(3)
    second(2)
    late = [mine(4)] + [other(z) for z in (1, 7, 2, 6, 3, 5, 4)]
    for n in range(4, 8):
        slots = late[2 * n - 8 : 2 * n - 6]
        for slot in slots[1 if n == 4 else 0 :]:
            arrive(cells(slot), t_recv.at[slot])
        operand(n, slots)
        first(n)
        second(n - 1)
    second(7)
    lsend[...] = combine([lpart[n] for n in range(8)])
    for n, offset in enumerate(TGT_PEERS):
        to_t(offset, lsend, lrecv.at[me_t], l_send.at[n], l_recv)
    lrecv[me_t] = lsend[...]

    for p in range(8):
        at = slice(128 * p, 128 * p + 128)
        xt[at, 0:128] = jnp.transpose(xr[0:128, at].astype(F32)).astype(BF16)
    for q in range(13):
        at = slice(128 * q, 128 * q + 128)
        lane = lane_iota(40)
        block = None
        for shard, offset, start, stop in column_pieces(q):
            piece = trecv[shard]
            shift = (start - offset) % 128
            if shift:
                piece = pltpu.roll(piece, shift, 1)
            block = piece if block is None else jnp.where(lane >= start, piece, block)
        y1, y2, y3 = split3(block[0:DIM])
        tlw[q : q + 1, :] = block[DIM + 1 : DIM + 2]
        yr[0:128, at] = jnp.concatenate([y1, y2, y1, y2], 0).astype(BF16)
        yr[128:192, at] = jnp.concatenate([y3, y1], 0).astype(BF16)
        yr[192:208, at] = ones16
        yr[208:256, at] = zeros48
        yt[at, 0:128] = jnp.transpose(jnp.concatenate([y1, y2, y1, y2], 0)).astype(BF16)
        tl[0:32, at] = y1.astype(BF16)
        tl[32:48, at] = jnp.ones((16, 128), BF16)
        tl[48:80, at] = y2.astype(BF16)

    for offset in reversed(TGT_PEERS):
        slot = at_t(offset)
        arrive(lrecv.at[slot], l_recv.at[slot])
    row_lse = combine([lrecv[k] for k in range(GROUP)])
    lall[...] = row_lse
    for p in range(8):
        at = slice(128 * p, 128 * p + 128)
        bias = slw[p : p + 1, :] - row_lse[p : p + 1, :]
        tail = jnp.concatenate([xr[128:192, at].astype(F32), bias_rows(bias), zeros56], 0)
        xt[at, 128:256] = jnp.transpose(tail).astype(BF16)

    jobs = [
        (half, base, start, min(256, count - start))
        for half, (base, count) in enumerate(HALVES)
        for start in range(0, count, 256)
    ]

    def first(n):
        half, base, start, width = jobs[n]
        scores = dot(xt[...], yr[:, base + start : base + start + width])
        scr[n % 2, :, 0:width] = scores
        peak[n % 2, :, 0:width] = jnp.max(scores, 0, keepdims=True)

    def second(n):
        half, base, start, width = jobs[n]
        top = peak[n % 2, :, 0:width]
        part = top + jnp.log(
            jnp.sum(jnp.exp2(scr[n % 2, :, 0:width] - top), 0, keepdims=True)
        ) * LOG2E
        for h in range(width // 128):
            line = start // 128 + h
            csend[half, line : line + 1, :] = part[:, 128 * h : 128 * h + 128]

    lines = [count // 128 for base, count in HALVES]

    def to_partner(half):
        there = crecv.at[half, 0 : lines[half]]
        copy = pltpu.make_async_remote_copy(
            src_ref=csend.at[half, 0 : lines[half]], dst_ref=there,
            send_sem=c_send.at[half], recv_sem=c_recv.at[half],
            device_id={"src": at_s((0, 1))}, device_id_type=MESH,
        )
        copy.start()
        sent.append(copy)

    def to_line(half):
        there = crecv.at[half, 0 : lines[half]]
        arrive(there, c_recv.at[half])
        gsend[half] = combine([csend[half], crecv[half]])
        for n, z in enumerate(Z_PEERS):
            to_s((z, 0), half * 8 + me_z, gsend.at[half, 0 : lines[half]],
                 grecv.at[half, me_z, 0 : lines[half]], g_send.at[half * 8 + n], g_recv)
        grecv[half, me_z] = gsend[half]

    for n in range(len(jobs) + 1):
        if n < len(jobs):
            first(n)
        if n > 0:
            second(n - 1)
            if n == 3:
                to_partner(0)
            if n == 5:
                to_line(0)
    to_partner(1)
    to_line(1)

    row = lall[pl.ds(me_y * 2 + me_x // 2, 1), :]
    row = jnp.where(lax.rem(me_t, 2) == 1, pltpu.roll(row, 64, 1), row)
    f_ref[...] = (src_sq - (EPSILON / LOG2E) * row)[:, 0:OWN_ROWS]

    for half, (base, count) in enumerate(HALVES):
        for z in reversed(Z_PEERS):
            slot = lax.rem(me_z + z, 8)
            arrive(grecv.at[half, slot, 0 : lines[half]], g_recv.at[half * 8 + slot])
        col_lse = combine([grecv[half, k] for k in range(8)])
        gall[base // 128 : base // 128 + lines[half], :] = col_lse[0 : lines[half]]
        for line in range(lines[half]):
            at = slice(base + 128 * line, base + 128 * line + 128)
            q = base // 128 + line
            bias = tlw[q : q + 1, :] - col_lse[line : line + 1, :]
            tail = jnp.concatenate([yr[128:192, at].astype(F32), bias_rows(bias), zeros56], 0)
            yt[at, 128:256] = jnp.transpose(tail).astype(BF16)
        span = slice(base, base + count)
        orders = (2, 1, 3, 0)

        def first(n):
            columns = pl.ds(pl.multiple_of(lax.rem(me_y + orders[n], 4) * 256, 256), 256)
            scores = dot(yt[span, :], xr[:, columns])
            scr[n % 2, 0:count, :] = scores
            peak[n % 2, :, 0:256] = jnp.max(scores, 0, keepdims=True)

        def second(n):
            order = orders[n]
            tile = lax.rem(me_y + order, 4)
            top = peak[n % 2, :, 0:256]
            weights = jnp.exp2(scr[n % 2, 0:count, :] - top)
            high = weights.astype(BF16)
            rest = (weights - high.astype(F32)).astype(BF16)
            main = dot(tl[0:80, span], high)
            moments = jnp.concatenate(
                [main[0:32] + main[48:80], main[32:40]], 0
            ) + dot(tl[0:48, span], rest)[0:40]
            if half == 0:
                moms[n] = moments
                tops[n] = jnp.broadcast_to(top, (8, 256))
                return
            before = tops[n]
            both = jnp.maximum(before, top)
            fix_a, fix_b = jnp.exp2(before - both), jnp.exp2(top - both)
            moments = moms[n] * fix_a[0:1] + moments * fix_b[0:1]
            for u in range(4):
                lanes = slice(128 * (u // 2), 128 * (u // 2) + 128)
                one, two = moments[0:16, lanes], moments[16:32, lanes]
                three, four = moments[32:40, lanes], both[:, lanes]
                if u % 2 == 0:
                    two, four = pltpu.roll(two, 64, 1), pltpu.roll(four, 64, 1)
                else:
                    one, three = pltpu.roll(one, 64, 1), pltpu.roll(three, 64, 1)
                msend[tile * 4 + u, 0:16, :] = jnp.where(low, one, two)
                msend[tile * 4 + u, 16:24, :] = jnp.where(low[0:8], three, four)
            for x in range(0 if order else 1, 4):
                slot = tile * 4 + lax.rem(me_x + x, 4)
                to_t((order, x), msend.at[slot, 0:SRC_LINES], mrecv.at[me_t, 0:SRC_LINES],
                     m_send.at[order * 4 + x], m_recv)

        for n in range(5):
            if n < 4:
                first(n)
            if n > 0:
                second(n - 1)
    mrecv[me_t] = msend[me_t]

    start = me_s * OWN_COLS
    line, offset = start // 128, lax.rem(start, 128)
    here = pltpu.roll(gall[pl.ds(line, 1), :], 128 - offset, 1)
    after = pltpu.roll(gall[pl.ds(line + 1, 1), :], 128 - offset, 1)
    col = jnp.where(lane_iota(1) < 128 - offset, here, after)
    g_ref[...] = (tgt_sq - (EPSILON / LOG2E) * col)[:, 0:OWN_COLS]

    for offset in reversed(TGT_PEERS):
        slot = at_t(offset)
        arrive(mrecv.at[slot, 0:SRC_LINES], m_recv.at[slot])
    top = mrecv[0, 16:17, :]
    for k in range(1, GROUP):
        top = jnp.maximum(top, mrecv[k, 16:17, :])
    acc, norm = jnp.zeros((16, 128), F32), jnp.zeros((1, 128), F32)
    low1 = low[0:1]
    for k in range(GROUP):
        last = mrecv[k, 16:17, :]
        fix = jnp.exp2(last - top)
        fix = jnp.where(low1, pltpu.roll(fix, 64, 1), fix)
        acc = acc + mrecv[k, 0:16, :] * fix
        norm = norm + last * fix
    ratio = acc / jnp.where(low1, norm, pltpu.roll(norm, 64, 1))
    p_ref[0:16, :] = ratio[:, 0:OWN_ROWS]
    p_ref[16:32, :] = pltpu.roll(ratio, 64, 1)[:, 0:OWN_ROWS]
    for copy in sent:
        copy.wait_send()


def body(source, target, target_pot, source_logw, target_logw):
    vmem = pl.BlockSpec(memory_space=pltpu.VMEM)
    f_new, g_new, projection = pl.pallas_call(
        kernel,
        out_shape=(
            jax.ShapeDtypeStruct((1, OWN_ROWS), F32),
            jax.ShapeDtypeStruct((1, OWN_COLS), F32),
            jax.ShapeDtypeStruct((DIM, OWN_ROWS), F32),
        ),
        in_specs=[pl.BlockSpec(memory_space=pl.ANY)] * 5,
        out_specs=(vmem,) * 3,
        scratch_shapes=[
            pltpu.VMEM((DIM, OWN_ROWS), F32),
            pltpu.VMEM((DIM, OWN_COLS), F32),
            pltpu.VMEM((1, OWN_COLS), F32),
            pltpu.VMEM((1, OWN_ROWS), F32),
            pltpu.VMEM((1, OWN_COLS), F32),
            pltpu.VMEM((40, 128), F32),
            pltpu.VMEM((24, 128), F32),
            pltpu.VMEM((40, 128), F32),
            pltpu.VMEM((GROUP, 24, 128), F32),
            pltpu.VMEM((GROUP, 40, 128), F32),
            pltpu.VMEM((256, ROWS), BF16),
            pltpu.VMEM((256, COLS), BF16),
            pltpu.VMEM((ROWS, 256), BF16),
            pltpu.VMEM((COLS, 256), BF16),
            pltpu.VMEM((80, COLS), BF16),
            pltpu.VMEM((8, 2 * OWN_COLS, 256), BF16),
            pltpu.VMEM((2, 2 * OWN_COLS, ROWS), F32),
            pltpu.VMEM((2, 1, ROWS), F32),
            pltpu.VMEM((2, ROWS, 256), F32),
            pltpu.VMEM((8, 128), F32),
            pltpu.VMEM((16, 128), F32),
            pltpu.VMEM((8, 8, 128), F32),
            pltpu.VMEM((8, 128), F32),
            pltpu.VMEM((GROUP, 8, 128), F32),
            pltpu.VMEM((2, 8, 128), F32),
            pltpu.VMEM((2, 8, 128), F32),
            pltpu.VMEM((2, 8, 128), F32),
            pltpu.VMEM((2, 8, 8, 128), F32),
            pltpu.VMEM((4, 40, 256), F32),
            pltpu.VMEM((4, 8, 256), F32),
            pltpu.VMEM((GROUP, 24, 128), F32),
            pltpu.VMEM((GROUP, 24, 128), F32),
            pltpu.VMEM((8, 128), F32),
            pltpu.VMEM((16, 128), F32),
            pltpu.SemaphoreType.DMA((5,)),
        ]
        + [pltpu.SemaphoreType.DMA((GROUP,))] * 6
        + [pltpu.SemaphoreType.DMA((GROUP,))] * 4
        + [pltpu.SemaphoreType.DMA((2,))] * 2,
        compiler_params=pltpu.CompilerParams(
            collective_id=0, has_side_effects=True, vmem_limit_bytes=60 * 1024 * 1024
        ),
    )(
        source,
        target,
        target_pot.reshape(1, OWN_COLS),
        source_logw.reshape(1, OWN_ROWS),
        target_logw.reshape(1, OWN_COLS),
    )
    return f_new.reshape(OWN_ROWS), g_new.reshape(OWN_COLS), projection


def solution(mesh):
    return jax.shard_map(
        body,
        mesh=mesh,
        in_specs=(
            P(None, ("src", "tgt")),
            P(None, ("tgt", "src")),
            P(("tgt", "src")),
            P(("src", "tgt")),
            P(("tgt", "src")),
        ),
        out_specs=(P(("src", "tgt")), P(("tgt", "src")), P(None, ("src", "tgt"))),
        check_vma=False,
    )
```

```python
import math

import jax
import jax.numpy as jnp
from jax import lax
from jax.experimental import pallas as pl
from jax.experimental.pallas import tpu as pltpu
from jax.sharding import PartitionSpec as P

EPSILON = 0.05
LOG2E = 1.0 / math.log(2.0)
SCALE = LOG2E / EPSILON
F32 = jnp.float32
BF16 = jnp.bfloat16
MESH = pl.DeviceIdType.MESH
GROUP = 16
ROWS = 1024
COLS = 1664
OWN_ROWS = 64
OWN_COLS = 104
DIM = 32
SRC_LINES = 17
TGT_LINES = 34


def ring(d, n):
    return min(d, n - d)


TGT_PEERS = sorted(
    [(y, x) for y in range(4) for x in range(4) if y or x],
    key=lambda o: -(ring(o[0], 4) + ring(o[1], 4)),
)
Z_PEERS = (4, 3, 5, 2, 6, 1, 7)
Z_NEAR = (1, 7, 2, 6)
Z_FAR = (3, 5, 4)


def dot(a, b):
    return lax.dot_general(a, b, (((1,), (0,)), ((), ())), preferred_element_type=F32)


def split3(x):
    one = x.astype(BF16).astype(F32)
    rest = x - one
    two = rest.astype(BF16).astype(F32)
    return one, two, rest - two


def lane_iota(rows):
    return lax.broadcasted_iota(jnp.int32, (rows, 128), 1)


def sub_iota(rows):
    return lax.broadcasted_iota(jnp.int32, (rows, 128), 0)


def bias_rows(bias):
    one, two, three = split3(bias)
    sub = sub_iota(8)
    return jnp.where(sub == 0, one, jnp.where(sub == 1, two, jnp.where(sub == 2, three, 0.0)))


def combine(parts):
    top = parts[0]
    for part in parts[1:]:
        top = jnp.maximum(top, part)
    total = jnp.exp2(parts[0] - top)
    for part in parts[1:]:
        total = total + jnp.exp2(part - top)
    return top + jnp.log(total) * LOG2E


def column_pieces(block):
    start, pieces = block * 128, []
    while start < block * 128 + 128:
        shard, offset = divmod(start, OWN_COLS)
        stop = min((shard + 1) * OWN_COLS, block * 128 + 128)
        pieces.append((shard, offset, start - block * 128, stop - block * 128))
        start = stop
    return pieces


def lse(scores):
    top = jnp.max(scores, 0, keepdims=True)
    return top + jnp.log(jnp.sum(jnp.exp2(scores - top), 0, keepdims=True)) * LOG2E


def kernel(
    src_hbm, tgt_hbm, pot_hbm, slw_hbm, tlw_hbm,
    f_ref, g_ref, p_ref,
    src_v, tgt_v, pot_v, slw_v, tlw_v,
    pad, smsg, tmsg, srecv, trecv,
    xr, yr, xt, yt, tl, ya, held, peak, scr,
    slw, tlw, lpart, lsend, lrecv, csend, crecv, gsend, grecv, msend, mrecv, lall, gall,
    in_sem, s_send, s_recv, t_send, t_recv, l_send, l_recv, g_send, g_recv, m_send, m_recv, c_send, c_recv,
):
    me_t = lax.axis_index("tgt")
    me_s = lax.axis_index("src")
    me_y, me_x = me_t // 4, lax.rem(me_t, 4)
    me_z, me_c = me_s // 2, lax.rem(me_s, 2)

    def at_t(offset):
        return lax.rem(me_y + offset[0], 4) * 4 + lax.rem(me_x + offset[1], 4)

    def at_s(offset):
        return lax.rem(me_z + offset[0], 8) * 2 + lax.rem(me_c + offset[1], 2)

    barrier = pltpu.get_barrier_semaphore()
    for offset in TGT_PEERS:
        pl.semaphore_signal(barrier, inc=1, device_id={"tgt": at_t(offset)}, device_id_type=MESH)
    for offset in [(z, 0) for z in Z_PEERS] + [(0, 1)]:
        pl.semaphore_signal(barrier, inc=1, device_id={"src": at_s(offset)}, device_id_type=MESH)

    inputs = [
        pltpu.make_async_copy(a, b, in_sem.at[n])
        for n, (a, b) in enumerate(
            ((src_hbm, src_v), (slw_hbm, slw_v), (tgt_hbm, tgt_v), (pot_hbm, pot_v), (tlw_hbm, tlw_v))
        )
    ]
    for copy in inputs:
        copy.start()
    pad[...] = jnp.zeros_like(pad)
    tmsg[...] = jnp.zeros_like(tmsg)
    low = lane_iota(16) < 64
    for copy in inputs:
        copy.wait()

    pad[0:DIM, 0:OWN_ROWS] = src_v[...]
    pad[DIM : DIM + 1, 0:OWN_ROWS] = slw_v[...] * LOG2E
    own = pad[...]
    src_sq = jnp.sum(own[0:DIM] * own[0:DIM], 0, keepdims=True)
    smsg[0:16, :] = jnp.where(low, own[0:16], pltpu.roll(own[16:32], 64, 1))
    smsg[16:24, :] = own[32:40]
    tmsg[0:DIM, 0:OWN_COLS] = tgt_v[...]
    own_t = tmsg[0:DIM, :]
    tgt_sq = jnp.sum(own_t * own_t, 0, keepdims=True)
    tmsg[DIM : DIM + 1, 0:OWN_COLS] = (
        SCALE * (pot_v[...] - tgt_sq[:, 0:OWN_COLS]) + LOG2E * tlw_v[...]
    )
    tmsg[DIM + 1 : DIM + 2, 0:OWN_COLS] = LOG2E * tlw_v[...]

    pl.semaphore_wait(barrier, len(TGT_PEERS) + len(Z_PEERS) + 1)
    sent = []

    def to_t(offset, src, dst, send, recv):
        copy = pltpu.make_async_remote_copy(
            src_ref=src, dst_ref=dst, send_sem=send, recv_sem=recv.at[me_t],
            device_id={"tgt": at_t(offset)}, device_id_type=MESH,
        )
        copy.start()
        sent.append(copy)

    def to_s(offset, slot, src, dst, send, recv):
        copy = pltpu.make_async_remote_copy(
            src_ref=src, dst_ref=dst, send_sem=send, recv_sem=recv.at[slot],
            device_id={"src": at_s(offset)}, device_id_type=MESH,
        )
        copy.start()
        sent.append(copy)

    def arrive(dst, sem):
        pltpu.make_async_copy(dst, dst, sem).wait()

    tgt_own = tmsg.at[0:TGT_LINES]
    for n, z in enumerate(Z_PEERS):
        to_s((z, 0), me_s, tgt_own, trecv.at[me_s, 0:TGT_LINES], t_send.at[n], t_recv)
    to_s((0, 1), me_s, tgt_own, trecv.at[me_s, 0:TGT_LINES], t_send.at[7], t_recv)
    src_own = smsg.at[0:SRC_LINES]
    for n, offset in enumerate(TGT_PEERS):
        to_t(offset, src_own, srecv.at[me_t, 0:SRC_LINES], s_send.at[n], s_recv)
    srecv[me_t] = smsg[...]
    trecv[me_s] = tmsg[...]
    ones16 = jnp.where(sub_iota(16) < 3, 1.0, 0.0).astype(BF16)
    zeros48 = jnp.zeros((48, 128), BF16)
    zeros56 = jnp.zeros((56, 128), F32)

    partner = lax.rem(me_c + 1, 2)

    def cells(slot):
        return trecv.at[slot, 0:TGT_LINES]

    def forward(n, z):
        slot = lax.rem(me_z + z, 8) * 2 + me_c
        arrive(cells(slot), t_recv.at[slot])
        to_s((0, 1), slot, cells(slot), cells(slot), t_send.at[8 + n], t_recv)

    def operand(n, slots):
        tops_t, tails_t = [], []
        for slot in slots:
            block = trecv[slot]
            y1, y2, y3 = split3(block[0:DIM])
            tops_t.append(jnp.transpose(jnp.concatenate([y1, y2, y1, y2], 0))[0:OWN_COLS])
            tail = jnp.concatenate([y3, y1, bias_rows(block[DIM : DIM + 1]), zeros56], 0)
            tails_t.append(jnp.transpose(tail)[0:OWN_COLS])
        ya[n, :, 0:128] = jnp.concatenate(tops_t, 0).astype(BF16)
        ya[n, :, 128:256] = jnp.concatenate(tails_t, 0).astype(BF16)

    def mine(z):
        return lax.rem(me_z + z, 8) * 2 + me_c

    def other(z):
        return lax.rem(me_z + z, 8) * 2 + partner

    def first(n):
        scores = dot(ya[n], xr[...])
        held[n % 2] = scores
        peak[n % 2] = jnp.max(scores, 0, keepdims=True)

    def second(n):
        top = peak[n % 2]
        part = top + jnp.log(jnp.sum(jnp.exp2(held[n % 2] - top), 0, keepdims=True)) * LOG2E
        for p in range(8):
            lpart[n, p : p + 1, :] = part[:, 128 * p : 128 * p + 128]

    arrive(cells(other(0)), t_recv.at[other(0)])
    operand(0, (me_s, other(0)))
    for n, z in enumerate(Z_NEAR):
        forward(n, z)
    operand(1, (mine(1), mine(7)))
    operand(2, (mine(2), mine(6)))

    for offset in reversed(TGT_PEERS):
        slot = at_t(offset)
        arrive(srecv.at[slot, 0:SRC_LINES], s_recv.at[slot])
    for p in range(8):
        a, b = srecv[2 * p], srecv[2 * p + 1]
        one = jnp.where(low, a[0:16], pltpu.roll(b[0:16], 64, 1))
        two = jnp.where(low, pltpu.roll(a[0:16], 64, 1), b[0:16])
        x1, x2, x3 = split3(jnp.concatenate([one, two], 0) * (2.0 * SCALE))
        at = slice(128 * p, 128 * p + 128)
        slw[p : p + 1, :] = jnp.where(low[0:1], a[16:17], pltpu.roll(b[16:24], 64, 1)[0:1])
        xr[0:128, at] = jnp.concatenate([x1, x1, x2, x2], 0).astype(BF16)
        xr[128:192, at] = jnp.concatenate([x1, x3], 0).astype(BF16)
        xr[192:208, at] = ones16
        xr[208:256, at] = zeros48
    for n, z in enumerate(Z_FAR):
        forward(4 + n, z)
    operand(3, (mine(3), mine(5)))
    first(0)
    first(1)
    second(0)
    first(2)
    second(1)
    first(3)
    second(2)
    late = [mine(4)] + [other(z) for z in (1, 7, 2, 6, 3, 5, 4)]
    for n in range(4, 8):
        slots = late[2 * n - 8 : 2 * n - 6]
        for slot in slots[1 if n == 4 else 0 :]:
            arrive(cells(slot), t_recv.at[slot])
        operand(n, slots)
        first(n)
        second(n - 1)
    second(7)
    lsend[...] = combine([lpart[n] for n in range(8)])
    for n, offset in enumerate(TGT_PEERS):
        to_t(offset, lsend, lrecv.at[me_t], l_send.at[n], l_recv)
    lrecv[me_t] = lsend[...]

    for p in range(8):
        at = slice(128 * p, 128 * p + 128)
        xt[at, 0:128] = jnp.transpose(xr[0:128, at].astype(F32)).astype(BF16)
    for q in range(13):
        at = slice(128 * q, 128 * q + 128)
        lane = lane_iota(40)
        block = None
        for shard, offset, start, stop in column_pieces(q):
            piece = trecv[shard]
            shift = (start - offset) % 128
            if shift:
                piece = pltpu.roll(piece, shift, 1)
            block = piece if block is None else jnp.where(lane >= start, piece, block)
        y1, y2, y3 = split3(block[0:DIM])
        tlw[q : q + 1, :] = block[DIM + 1 : DIM + 2]
        yr[0:128, at] = jnp.concatenate([y1, y2, y1, y2], 0).astype(BF16)
        yr[128:192, at] = jnp.concatenate([y3, y1], 0).astype(BF16)
        yr[192:208, at] = ones16
        yr[208:256, at] = zeros48
        yt[at, 0:128] = jnp.transpose(jnp.concatenate([y1, y2, y1, y2], 0)).astype(BF16)
        tl[0:32, at] = y1.astype(BF16)
        tl[32:48, at] = jnp.ones((16, 128), BF16)
        tl[48:80, at] = y2.astype(BF16)

    for offset in reversed(TGT_PEERS):
        slot = at_t(offset)
        arrive(lrecv.at[slot], l_recv.at[slot])
    row_lse = combine([lrecv[k] for k in range(GROUP)])
    lall[...] = row_lse
    for p in range(8):
        at = slice(128 * p, 128 * p + 128)
        bias = slw[p : p + 1, :] - row_lse[p : p + 1, :]
        tail = jnp.concatenate([xr[128:192, at].astype(F32), bias_rows(bias), zeros56], 0)
        xt[at, 128:256] = jnp.transpose(tail).astype(BF16)

    def first(n):
        width = min(256, COLS - 256 * n)
        scores = dot(xt[...], yr[:, 256 * n : 256 * n + width])
        scr[n % 2, 0:ROWS, 0:width] = scores
        peak[n % 2, :, 0:width] = jnp.max(scores, 0, keepdims=True)

    def second(n):
        width = min(256, COLS - 256 * n)
        top = peak[n % 2, :, 0:width]
        part = top + jnp.log(
            jnp.sum(jnp.exp2(scr[n % 2, 0:ROWS, 0:width] - top), 0, keepdims=True)
        ) * LOG2E
        for h in range(width // 128):
            csend[2 * n + h : 2 * n + h + 1, :] = part[:, 128 * h : 128 * h + 128]

    for n in range(8):
        if n < 7:
            first(n)
        if n > 0:
            second(n - 1)
    there = crecv.at[0:13]
    copy = pltpu.make_async_remote_copy(
        src_ref=csend.at[0:13], dst_ref=there, send_sem=c_send.at[0], recv_sem=c_recv.at[0],
        device_id={"src": at_s((0, 1))}, device_id_type=MESH,
    )
    copy.start()
    sent.append(copy)
    arrive(there, c_recv.at[0])
    gsend[...] = combine([csend[...], crecv[...]])
    for n, z in enumerate(Z_PEERS):
        to_s((z, 0), me_z, gsend.at[0:13], grecv.at[me_z, 0:13], g_send.at[n], g_recv)
    grecv[me_z] = gsend[...]

    row = lall[pl.ds(me_y * 2 + me_x // 2, 1), :]
    row = jnp.where(lax.rem(me_t, 2) == 1, pltpu.roll(row, 64, 1), row)
    f_ref[...] = (src_sq - (EPSILON / LOG2E) * row)[:, 0:OWN_ROWS]

    for z in reversed(Z_PEERS):
        slot = lax.rem(me_z + z, 8)
        arrive(grecv.at[slot, 0:13], g_recv.at[slot])
    col_lse = combine([grecv[k] for k in range(8)])
    gall[...] = col_lse
    for q in range(13):
        at = slice(128 * q, 128 * q + 128)
        bias = tlw[q : q + 1, :] - col_lse[q : q + 1, :]
        tail = jnp.concatenate([yr[128:192, at].astype(F32), bias_rows(bias), zeros56], 0)
        yt[at, 128:256] = jnp.transpose(tail).astype(BF16)
    orders = (2, 1, 3, 0)

    def first(n):
        columns = pl.ds(pl.multiple_of(lax.rem(me_y + orders[n], 4) * 256, 256), 256)
        scores = dot(yt[...], xr[:, columns])
        scr[n % 2] = scores
        peak[n % 2, :, 0:256] = jnp.max(scores, 0, keepdims=True)

    def second(n):
        order = orders[n]
        tile = lax.rem(me_y + order, 4)
        top = peak[n % 2, :, 0:256]
        weights = jnp.exp2(scr[n % 2] - top)
        high = weights.astype(BF16)
        rest = (weights - high.astype(F32)).astype(BF16)
        main = dot(tl[...], high)
        moments = jnp.concatenate([main[0:32] + main[48:80], main[32:40]], 0) + dot(tl[0:48, :], rest)[0:40]
        for u in range(4):
            lanes = slice(128 * (u // 2), 128 * (u // 2) + 128)
            one, two = moments[0:16, lanes], moments[16:32, lanes]
            three, four = moments[32:40, lanes], jnp.broadcast_to(top[:, lanes], (8, 128))
            if u % 2 == 0:
                two, four = pltpu.roll(two, 64, 1), pltpu.roll(four, 64, 1)
            else:
                one, three = pltpu.roll(one, 64, 1), pltpu.roll(three, 64, 1)
            msend[tile * 4 + u, 0:16, :] = jnp.where(low, one, two)
            msend[tile * 4 + u, 16:24, :] = jnp.where(low[0:8], three, four)
        for x in range(0 if order else 1, 4):
            slot = tile * 4 + lax.rem(me_x + x, 4)
            to_t((order, x), msend.at[slot, 0:SRC_LINES], mrecv.at[me_t, 0:SRC_LINES],
                 m_send.at[order * 4 + x], m_recv)

    for n in range(5):
        if n < 4:
            first(n)
        if n > 0:
            second(n - 1)
    mrecv[me_t] = msend[me_t]

    start = me_s * OWN_COLS
    line, offset = start // 128, lax.rem(start, 128)
    here = pltpu.roll(gall[pl.ds(line, 1), :], 128 - offset, 1)
    after = pltpu.roll(gall[pl.ds(line + 1, 1), :], 128 - offset, 1)
    col = jnp.where(lane_iota(1) < 128 - offset, here, after)
    g_ref[...] = (tgt_sq - (EPSILON / LOG2E) * col)[:, 0:OWN_COLS]

    for offset in reversed(TGT_PEERS):
        slot = at_t(offset)
        arrive(mrecv.at[slot, 0:SRC_LINES], m_recv.at[slot])
    top = mrecv[0, 16:17, :]
    for k in range(1, GROUP):
        top = jnp.maximum(top, mrecv[k, 16:17, :])
    acc, norm = jnp.zeros((16, 128), F32), jnp.zeros((1, 128), F32)
    low1 = low[0:1]
    for k in range(GROUP):
        last = mrecv[k, 16:17, :]
        fix = jnp.exp2(last - top)
        fix = jnp.where(low1, pltpu.roll(fix, 64, 1), fix)
        acc = acc + mrecv[k, 0:16, :] * fix
        norm = norm + last * fix
    ratio = acc / jnp.where(low1, norm, pltpu.roll(norm, 64, 1))
    p_ref[0:16, :] = ratio[:, 0:OWN_ROWS]
    p_ref[16:32, :] = pltpu.roll(ratio, 64, 1)[:, 0:OWN_ROWS]
    for copy in sent:
        copy.wait_send()


def body(source, target, target_pot, source_logw, target_logw):
    vmem = pl.BlockSpec(memory_space=pltpu.VMEM)
    f_new, g_new, projection = pl.pallas_call(
        kernel,
        out_shape=(
            jax.ShapeDtypeStruct((1, OWN_ROWS), F32),
            jax.ShapeDtypeStruct((1, OWN_COLS), F32),
            jax.ShapeDtypeStruct((DIM, OWN_ROWS), F32),
        ),
        in_specs=[pl.BlockSpec(memory_space=pl.ANY)] * 5,
        out_specs=(vmem,) * 3,
        scratch_shapes=[
            pltpu.VMEM((DIM, OWN_ROWS), F32),
            pltpu.VMEM((DIM, OWN_COLS), F32),
            pltpu.VMEM((1, OWN_COLS), F32),
            pltpu.VMEM((1, OWN_ROWS), F32),
            pltpu.VMEM((1, OWN_COLS), F32),
            pltpu.VMEM((40, 128), F32),
            pltpu.VMEM((24, 128), F32),
            pltpu.VMEM((40, 128), F32),
            pltpu.VMEM((GROUP, 24, 128), F32),
            pltpu.VMEM((GROUP, 40, 128), F32),
            pltpu.VMEM((256, ROWS), BF16),
            pltpu.VMEM((256, COLS), BF16),
            pltpu.VMEM((ROWS, 256), BF16),
            pltpu.VMEM((COLS, 256), BF16),
            pltpu.VMEM((80, COLS), BF16),
            pltpu.VMEM((8, 2 * OWN_COLS, 256), BF16),
            pltpu.VMEM((2, 2 * OWN_COLS, ROWS), F32),
            pltpu.VMEM((2, 1, ROWS), F32),
            pltpu.VMEM((2, COLS, 256), F32),
            pltpu.VMEM((8, 128), F32),
            pltpu.VMEM((16, 128), F32),
            pltpu.VMEM((8, 8, 128), F32),
            pltpu.VMEM((8, 128), F32),
            pltpu.VMEM((GROUP, 8, 128), F32),
            pltpu.VMEM((16, 128), F32),
            pltpu.VMEM((16, 128), F32),
            pltpu.VMEM((16, 128), F32),
            pltpu.VMEM((8, 16, 128), F32),
            pltpu.VMEM((GROUP, 24, 128), F32),
            pltpu.VMEM((GROUP, 24, 128), F32),
            pltpu.VMEM((8, 128), F32),
            pltpu.VMEM((16, 128), F32),
            pltpu.SemaphoreType.DMA((5,)),
        ]
        + [pltpu.SemaphoreType.DMA((GROUP,))] * 6
        + [pltpu.SemaphoreType.DMA((GROUP,))] * 4
        + [pltpu.SemaphoreType.DMA((1,))] * 2,
        compiler_params=pltpu.CompilerParams(
            collective_id=0, has_side_effects=True, vmem_limit_bytes=60 * 1024 * 1024
        ),
    )(
        source,
        target,
        target_pot.reshape(1, OWN_COLS),
        source_logw.reshape(1, OWN_ROWS),
        target_logw.reshape(1, OWN_COLS),
    )
    return f_new.reshape(OWN_ROWS), g_new.reshape(OWN_COLS), projection


def solution(mesh):
    return jax.shard_map(
        body,
        mesh=mesh,
        in_specs=(
            P(None, ("src", "tgt")),
            P(None, ("tgt", "src")),
            P(("tgt", "src")),
            P(("src", "tgt")),
            P(("tgt", "src")),
        ),
        out_specs=(P(("src", "tgt")), P(("tgt", "src")), P(None, ("src", "tgt"))),
        check_vma=False,
    )
```

```python
import math

import jax
import jax.numpy as jnp
from jax import lax
from jax.experimental import pallas as pl
from jax.experimental.pallas import tpu as pltpu
from jax.sharding import PartitionSpec as P

EPSILON = 0.05
LOG2E = 1.0 / math.log(2.0)
SCALE = LOG2E / EPSILON
TOP_LOGW = -9.0 * LOG2E
F32 = jnp.float32
BF16 = jnp.bfloat16
MESH = pl.DeviceIdType.MESH
GROUP = 16
ROWS = 1024
COLS = 1664
OWN_ROWS = 64
OWN_COLS = 104
DIM = 32
SRC_LINES = 17
TGT_LINES = 34


def ring(d, n):
    return min(d, n - d)


TGT_PEERS = sorted(
    [(y, x) for y in range(4) for x in range(4) if y or x],
    key=lambda o: -(ring(o[0], 4) + ring(o[1], 4)),
)
Z_PEERS = (4, 3, 5, 2, 6, 1, 7)


def dot(a, b):
    return lax.dot_general(a, b, (((1,), (0,)), ((), ())), preferred_element_type=F32)


def split3(x):
    one = x.astype(BF16).astype(F32)
    rest = x - one
    two = rest.astype(BF16).astype(F32)
    return one, two, rest - two


def lane_iota(rows):
    return lax.broadcasted_iota(jnp.int32, (rows, 128), 1)


def sub_iota(rows):
    return lax.broadcasted_iota(jnp.int32, (rows, 128), 0)


def bias_rows(bias, at=0, other=0.0):
    one, two, three = split3(bias)
    sub = sub_iota(8)
    rest = jnp.where(sub < 6, other, 0.0)
    return jnp.where(sub == at, one, jnp.where(sub == at + 1, two, jnp.where(sub == at + 2, three, rest)))


def combine(parts):
    top = parts[0]
    for part in parts[1:]:
        top = jnp.maximum(top, part)
    total = jnp.exp2(parts[0] - top)
    for part in parts[1:]:
        total = total + jnp.exp2(part - top)
    return top + jnp.log(total) * LOG2E


def column_pieces(block):
    start, pieces = block * 128, []
    while start < block * 128 + 128:
        shard, offset = divmod(start, OWN_COLS)
        stop = min((shard + 1) * OWN_COLS, block * 128 + 128)
        pieces.append((shard, offset, start - block * 128, stop - block * 128))
        start = stop
    return pieces


def lse(scores):
    top = jnp.max(scores, 0, keepdims=True)
    return top + jnp.log(jnp.sum(jnp.exp2(scores - top), 0, keepdims=True)) * LOG2E


def kernel(
    src_hbm, tgt_hbm, pot_hbm, slw_hbm, tlw_hbm,
    out_ref,
    src_v, tgt_v, pot_v, slw_v, tlw_v,
    pad, smsg, tmsg, srecv, trecv,
    xr, yr, xt, yt, tl, ya, held, peak, scr,
    slw, tlw, lpart, lsend, lrecv, csend, crecv, gsend, grecv, msend, mrecv, lall, gall,
    in_sem, s_send, s_recv, t_send, t_recv, l_send, l_recv, g_send, g_recv, m_send, m_recv, c_send, c_recv,
):
    me_t = lax.axis_index("tgt")
    me_s = lax.axis_index("src")
    me_y, me_x = me_t // 4, lax.rem(me_t, 4)
    me_z, me_c = me_s // 2, lax.rem(me_s, 2)

    def at_t(offset):
        return lax.rem(me_y + offset[0], 4) * 4 + lax.rem(me_x + offset[1], 4)

    def at_s(offset):
        return lax.rem(me_z + offset[0], 8) * 2 + lax.rem(me_c + offset[1], 2)

    barrier = pltpu.get_barrier_semaphore()
    for offset in TGT_PEERS:
        pl.semaphore_signal(barrier, inc=1, device_id={"tgt": at_t(offset)}, device_id_type=MESH)
    for offset in [(z, 0) for z in Z_PEERS] + [(0, 1)]:
        pl.semaphore_signal(barrier, inc=1, device_id={"src": at_s(offset)}, device_id_type=MESH)

    inputs = [
        pltpu.make_async_copy(a, b, in_sem.at[n])
        for n, (a, b) in enumerate(
            ((src_hbm, src_v), (slw_hbm, slw_v), (tgt_hbm, tgt_v), (pot_hbm, pot_v), (tlw_hbm, tlw_v))
        )
    ]
    for copy in inputs:
        copy.start()
    pad[...] = jnp.zeros_like(pad)
    tmsg[...] = jnp.zeros_like(tmsg)
    low = lane_iota(16) < 64
    for copy in inputs:
        copy.wait()

    pad[0:DIM, 0:OWN_ROWS] = src_v[...]
    pad[DIM : DIM + 1, 0:OWN_ROWS] = slw_v[...] * LOG2E
    own = pad[...]
    src_sq = jnp.sum(own[0:DIM] * own[0:DIM], 0, keepdims=True)
    smsg[0:16, :] = jnp.where(low, own[0:16], pltpu.roll(own[16:32], 64, 1))
    smsg[16:24, :] = own[32:40]
    tmsg[0:DIM, 0:OWN_COLS] = tgt_v[...]
    own_t = tmsg[0:DIM, :]
    tgt_sq = jnp.sum(own_t * own_t, 0, keepdims=True)
    tmsg[DIM : DIM + 1, 0:OWN_COLS] = (
        SCALE * (pot_v[...] - tgt_sq[:, 0:OWN_COLS]) + LOG2E * tlw_v[...]
    )
    tmsg[DIM + 1 : DIM + 2, 0:OWN_COLS] = LOG2E * tlw_v[...]

    pl.semaphore_wait(barrier, len(TGT_PEERS) + len(Z_PEERS) + 1)
    sent = []

    def to_t(offset, src, dst, send, recv):
        copy = pltpu.make_async_remote_copy(
            src_ref=src, dst_ref=dst, send_sem=send, recv_sem=recv.at[me_t],
            device_id={"tgt": at_t(offset)}, device_id_type=MESH,
        )
        copy.start()
        sent.append(copy)

    def to_s(offset, slot, src, dst, send, recv):
        copy = pltpu.make_async_remote_copy(
            src_ref=src, dst_ref=dst, send_sem=send, recv_sem=recv.at[slot],
            device_id={"src": at_s(offset)}, device_id_type=MESH,
        )
        copy.start()
        sent.append(copy)

    def arrive(dst, sem):
        pltpu.make_async_copy(dst, dst, sem).wait()

    tgt_own = tmsg.at[0:TGT_LINES]
    for n, z in enumerate(Z_PEERS):
        to_s((z, 0), 8 - z, tgt_own, trecv.at[0, 8 - z, 0:TGT_LINES], t_send.at[n], t_recv)
    src_own = smsg.at[0:SRC_LINES]
    for n, offset in enumerate(TGT_PEERS):
        to_t(offset, src_own, srecv.at[me_t, 0:SRC_LINES], s_send.at[n], s_recv)
    srecv[me_t] = smsg[...]
    trecv[0, 0] = tmsg[...]
    ones16 = jnp.where(sub_iota(16) < 3, 1.0, 0.0).astype(BF16)
    zeros48 = jnp.zeros((48, 128), BF16)
    zeros56 = jnp.zeros((56, 128), F32)

    def operand(n):
        tops_t, tails_t = [], []
        for z in (2 * n, 2 * n + 1):
            block = trecv[z // 8, z % 8]
            y1, y2, y3 = split3(block[0:DIM])
            tops_t.append(jnp.transpose(jnp.concatenate([y1, y2, y1, y2], 0))[0:OWN_COLS])
            tail = jnp.concatenate([y3, y1, bias_rows(block[DIM : DIM + 1]), zeros56], 0)
            tails_t.append(jnp.transpose(tail)[0:OWN_COLS])
        ya[n, :, 0:128] = jnp.concatenate(tops_t, 0).astype(BF16)
        ya[n, :, 128:256] = jnp.concatenate(tails_t, 0).astype(BF16)

    def first(n):
        scores = dot(ya[n], xr[...])
        held[n % 2] = scores
        peak[n % 2] = jnp.max(scores, 0, keepdims=True)

    def second(n):
        top = peak[n % 2]
        part = top + jnp.log(jnp.sum(jnp.exp2(held[n % 2] - top), 0, keepdims=True)) * LOG2E
        for p in range(8):
            lpart[n, p : p + 1, :] = part[:, 128 * p : 128 * p + 128]

    for z in reversed(Z_PEERS):
        arrive(trecv.at[0, 8 - z, 0:TGT_LINES], t_recv.at[8 - z])
    to_s((0, 1), 8, trecv.at[0, :, 0:TGT_LINES], trecv.at[1, :, 0:TGT_LINES], t_send.at[7], t_recv)
    operand(0)

    for offset in reversed(TGT_PEERS):
        slot = at_t(offset)
        arrive(srecv.at[slot, 0:SRC_LINES], s_recv.at[slot])
    for p in range(8):
        a, b = srecv[2 * p], srecv[2 * p + 1]
        one = jnp.where(low, a[0:16], pltpu.roll(b[0:16], 64, 1))
        two = jnp.where(low, pltpu.roll(a[0:16], 64, 1), b[0:16])
        x1, x2, x3 = split3(jnp.concatenate([one, two], 0) * (2.0 * SCALE))
        at = slice(128 * p, 128 * p + 128)
        slw[p : p + 1, :] = jnp.where(low[0:1], a[16:17], pltpu.roll(b[16:24], 64, 1)[0:1])
        xr[0:128, at] = jnp.concatenate([x1, x1, x2, x2], 0).astype(BF16)
        xr[128:192, at] = jnp.concatenate([x1, x3], 0).astype(BF16)
        xr[192:208, at] = ones16
        xr[208:256, at] = zeros48
    first(0)
    for n in range(1, 4):
        operand(n)
        first(n)
        second(n - 1)
    arrive(trecv.at[1, :, 0:TGT_LINES], t_recv.at[8])
    for n in range(4, 8):
        operand(n)
        first(n)
        second(n - 1)
    second(7)
    lsend[...] = combine([lpart[n] for n in range(8)])
    for n, offset in enumerate(TGT_PEERS):
        to_t(offset, lsend, lrecv.at[me_t], l_send.at[n], l_recv)
    lrecv[me_t] = lsend[...]

    for p in range(8):
        at = slice(128 * p, 128 * p + 128)
        xt[at, 0:128] = jnp.transpose(xr[0:128, at].astype(F32)).astype(BF16)
    for q in range(13):
        at = slice(128 * q, 128 * q + 128)
        lane = lane_iota(40)
        block = None
        for shard, offset, start, stop in column_pieces(q):
            piece = trecv[lax.rem(shard + me_c, 2), lax.rem(shard // 2 + 8 - me_z, 8)]
            shift = (start - offset) % 128
            if shift:
                piece = pltpu.roll(piece, shift, 1)
            block = piece if block is None else jnp.where(lane >= start, piece, block)
        y1, y2, y3 = split3(block[0:DIM])
        tlw[q : q + 1, :] = block[DIM + 1 : DIM + 2]
        yr[0:128, at] = jnp.concatenate([y1, y2, y1, y2], 0).astype(BF16)
        yr[128:192, at] = jnp.concatenate([y3, y1], 0).astype(BF16)
        yr[192:208, at] = ones16
        yr[208:256, at] = zeros48
        yt[at, 0:128] = jnp.transpose(jnp.concatenate([y1, y2, y1, y2], 0)).astype(BF16)
        tl[0:32, at] = y1.astype(BF16)
        tl[32:48, at] = jnp.ones((16, 128), BF16)
        tl[48:80, at] = y2.astype(BF16)

    for offset in reversed(TGT_PEERS):
        slot = at_t(offset)
        arrive(lrecv.at[slot], l_recv.at[slot])
    row_lse = combine([lrecv[k] for k in range(GROUP)])
    lall[...] = row_lse
    for p in range(8):
        at = slice(128 * p, 128 * p + 128)
        bias = slw[p : p + 1, :] - row_lse[p : p + 1, :]
        tail = jnp.concatenate([xr[128:192, at].astype(F32), bias_rows(bias), zeros56], 0)
        xt[at, 128:256] = jnp.transpose(tail).astype(BF16)
        both = jnp.concatenate([bias_rows(bias, 3, 1.0), jnp.zeros((8, 128), F32)], 0)
        xr[192:208, at] = both.astype(BF16)

    def first(n):
        width = min(256, COLS - 256 * n)
        scores = dot(xt[...], yr[:, 256 * n : 256 * n + width])
        scr[n % 2, 0:ROWS, 0:width] = scores
        peak[n % 2, :, 0:width] = jnp.max(scores, 0, keepdims=True)

    def second(n):
        width = min(256, COLS - 256 * n)
        top = peak[n % 2, :, 0:width]
        part = top + jnp.log(
            jnp.sum(jnp.exp2(scr[n % 2, 0:ROWS, 0:width] - top), 0, keepdims=True)
        ) * LOG2E
        for h in range(width // 128):
            csend[2 * n + h : 2 * n + h + 1, :] = part[:, 128 * h : 128 * h + 128]

    for n in range(8):
        if n < 7:
            first(n)
        if n > 0:
            second(n - 1)
    there = crecv.at[0:13]
    copy = pltpu.make_async_remote_copy(
        src_ref=csend.at[0:13], dst_ref=there, send_sem=c_send.at[0], recv_sem=c_recv.at[0],
        device_id={"src": at_s((0, 1))}, device_id_type=MESH,
    )
    copy.start()
    sent.append(copy)
    arrive(there, c_recv.at[0])
    gsend[...] = combine([csend[...], crecv[...]])
    for n, z in enumerate(Z_PEERS):
        to_s((z, 0), me_z, gsend.at[0:13], grecv.at[me_z, 0:13], g_send.at[n], g_recv)
    grecv[me_z] = gsend[...]

    row = lall[pl.ds(me_y * 2 + me_x // 2, 1), :]
    row = jnp.where(lax.rem(me_t, 2) == 1, pltpu.roll(row, 64, 1), row)
    out_ref[32:33, :] = src_sq - (EPSILON / LOG2E) * row

    for z in reversed(Z_PEERS):
        slot = lax.rem(me_z + z, 8)
        arrive(grecv.at[slot, 0:13], g_recv.at[slot])
    col_lse = combine([grecv[k] for k in range(8)])
    gall[...] = col_lse
    for q in range(13):
        at = slice(128 * q, 128 * q + 128)
        bias = tlw[q : q + 1, :] - col_lse[q : q + 1, :] - TOP_LOGW
        tail = jnp.concatenate([yr[128:192, at].astype(F32), bias_rows(bias, 0, 1.0), zeros56], 0)
        yt[at, 128:256] = jnp.transpose(tail).astype(BF16)
    spans = ((0, 512), (512, 1024), (1024, 1664))
    for order in (2, 1, 3, 0):
        tile = lax.rem(me_y + order, 4)
        columns = pl.ds(pl.multiple_of(tile * 256, 256), 256)
        moments = None
        for base, stop in spans:
            weights = jnp.exp2(dot(yt[base:stop, :], xr[:, columns]))
            high = weights.astype(BF16)
            rest = (weights - high.astype(F32)).astype(BF16)
            main = dot(tl[:, base:stop], high)
            part = jnp.concatenate([main[0:32] + main[48:80], main[32:40]], 0)
            part = part + dot(tl[0:48, base:stop], rest)[0:40]
            moments = part if moments is None else moments + part
        for u in range(4):
            lanes = slice(128 * (u // 2), 128 * (u // 2) + 128)
            one, two, three = moments[0:16, lanes], moments[16:32, lanes], moments[32:40, lanes]
            if u % 2 == 0:
                two = pltpu.roll(two, 64, 1)
            else:
                one, three = pltpu.roll(one, 64, 1), pltpu.roll(three, 64, 1)
            msend[tile * 4 + u, 0:16, :] = jnp.where(low, one, two)
            msend[tile * 4 + u, 16:24, :] = three
        for x in range(0 if order else 1, 4):
            slot = tile * 4 + lax.rem(me_x + x, 4)
            to_t((order, x), msend.at[slot, 0:SRC_LINES], mrecv.at[me_t, 0:SRC_LINES],
                 m_send.at[order * 4 + x], m_recv)
    mrecv[me_t] = msend[me_t]

    start = me_s * OWN_COLS
    line, offset = start // 128, lax.rem(start, 128)
    here = pltpu.roll(gall[pl.ds(line, 1), :], 128 - offset, 1)
    after = pltpu.roll(gall[pl.ds(line + 1, 1), :], 128 - offset, 1)
    col = jnp.where(lane_iota(1) < 128 - offset, here, after)
    out_ref[33:34, :] = tgt_sq - (EPSILON / LOG2E) * col
    out_ref[34:40, :] = jnp.zeros((6, 128), F32)

    for offset in reversed(TGT_PEERS):
        slot = at_t(offset)
        arrive(mrecv.at[slot, 0:SRC_LINES], m_recv.at[slot])
    acc, norm = mrecv[0, 0:16, :], mrecv[0, 16:17, :]
    for k in range(1, GROUP):
        acc = acc + mrecv[k, 0:16, :]
        norm = norm + mrecv[k, 16:17, :]
    ratio = acc / jnp.where(low[0:1], norm, pltpu.roll(norm, 64, 1))
    out_ref[0:16, :] = ratio
    out_ref[16:32, :] = pltpu.roll(ratio, 64, 1)
    for copy in sent:
        copy.wait_send()


def deliver(out_ref, f_ref, g_ref, p_ref):
    f_ref[...] = out_ref[32:33, 0:OWN_ROWS]
    g_ref[...] = out_ref[33:34, 0:OWN_COLS]
    p_ref[...] = out_ref[0:DIM, 0:OWN_ROWS]


def body(source, target, target_pot, source_logw, target_logw):
    vmem = pl.BlockSpec(memory_space=pltpu.VMEM)
    out = pl.pallas_call(
        kernel,
        out_shape=jax.ShapeDtypeStruct((40, 128), F32),
        in_specs=[pl.BlockSpec(memory_space=pl.ANY)] * 5,
        out_specs=vmem,
        scratch_shapes=[
            pltpu.VMEM((DIM, OWN_ROWS), F32),
            pltpu.VMEM((DIM, OWN_COLS), F32),
            pltpu.VMEM((1, OWN_COLS), F32),
            pltpu.VMEM((1, OWN_ROWS), F32),
            pltpu.VMEM((1, OWN_COLS), F32),
            pltpu.VMEM((40, 128), F32),
            pltpu.VMEM((24, 128), F32),
            pltpu.VMEM((40, 128), F32),
            pltpu.VMEM((GROUP, 24, 128), F32),
            pltpu.VMEM((2, 8, 40, 128), F32),
            pltpu.VMEM((256, ROWS), BF16),
            pltpu.VMEM((256, COLS), BF16),
            pltpu.VMEM((ROWS, 256), BF16),
            pltpu.VMEM((COLS, 256), BF16),
            pltpu.VMEM((80, COLS), BF16),
            pltpu.VMEM((8, 2 * OWN_COLS, 256), BF16),
            pltpu.VMEM((2, 2 * OWN_COLS, ROWS), F32),
            pltpu.VMEM((2, 1, ROWS), F32),
            pltpu.VMEM((2, COLS, 256), F32),
            pltpu.VMEM((8, 128), F32),
            pltpu.VMEM((16, 128), F32),
            pltpu.VMEM((8, 8, 128), F32),
            pltpu.VMEM((8, 128), F32),
            pltpu.VMEM((GROUP, 8, 128), F32),
            pltpu.VMEM((16, 128), F32),
            pltpu.VMEM((16, 128), F32),
            pltpu.VMEM((16, 128), F32),
            pltpu.VMEM((8, 16, 128), F32),
            pltpu.VMEM((GROUP, 24, 128), F32),
            pltpu.VMEM((GROUP, 24, 128), F32),
            pltpu.VMEM((8, 128), F32),
            pltpu.VMEM((16, 128), F32),
            pltpu.SemaphoreType.DMA((5,)),
        ]
        + [pltpu.SemaphoreType.DMA((GROUP,))] * 6
        + [pltpu.SemaphoreType.DMA((GROUP,))] * 4
        + [pltpu.SemaphoreType.DMA((1,))] * 2,
        compiler_params=pltpu.CompilerParams(
            collective_id=0, has_side_effects=True, vmem_limit_bytes=60 * 1024 * 1024
        ),
    )(
        source,
        target,
        target_pot.reshape(1, OWN_COLS),
        source_logw.reshape(1, OWN_ROWS),
        target_logw.reshape(1, OWN_COLS),
    )
    f_new, g_new, projection = pl.pallas_call(
        deliver,
        out_shape=(
            jax.ShapeDtypeStruct((1, OWN_ROWS), F32),
            jax.ShapeDtypeStruct((1, OWN_COLS), F32),
            jax.ShapeDtypeStruct((DIM, OWN_ROWS), F32),
        ),
        in_specs=[vmem],
        out_specs=(vmem,) * 3,
    )(out)
    return f_new.reshape(OWN_ROWS), g_new.reshape(OWN_COLS), projection


def solution(mesh):
    return jax.shard_map(
        body,
        mesh=mesh,
        in_specs=(
            P(None, ("src", "tgt")),
            P(None, ("tgt", "src")),
            P(("tgt", "src")),
            P(("src", "tgt")),
            P(("tgt", "src")),
        ),
        out_specs=(P(("src", "tgt")), P(("tgt", "src")), P(None, ("src", "tgt"))),
        check_vma=False,
    )
```

```python
import math

import jax
import jax.numpy as jnp
from jax import lax
from jax.experimental import pallas as pl
from jax.experimental.pallas import tpu as pltpu
from jax.sharding import PartitionSpec as P

EPSILON = 0.05
LOG2E = 1.0 / math.log(2.0)
SCALE = LOG2E / EPSILON
TOP_LOGW = -9.0 * LOG2E
F32 = jnp.float32
BF16 = jnp.bfloat16
MESH = pl.DeviceIdType.MESH
GROUP = 16
ROWS = 1024
COLS = 1664
OWN_ROWS = 64
OWN_COLS = 104
DIM = 32
SRC_LINES = 17
TGT_LINES = 34


def ring(d, n):
    return min(d, n - d)


TGT_PEERS = sorted(
    [(y, x) for y in range(4) for x in range(4) if y or x],
    key=lambda o: -(ring(o[0], 4) + ring(o[1], 4)),
)
Z_PEERS = (4, 3, 5, 2, 6, 1, 7)


def dot(a, b):
    return lax.dot_general(a, b, (((1,), (0,)), ((), ())), preferred_element_type=F32)


def split3(x):
    one = x.astype(BF16).astype(F32)
    rest = x - one
    two = rest.astype(BF16).astype(F32)
    return one, two, rest - two


def lane_iota(rows):
    return lax.broadcasted_iota(jnp.int32, (rows, 128), 1)


def sub_iota(rows):
    return lax.broadcasted_iota(jnp.int32, (rows, 128), 0)


def bias_rows(bias, at=0, other=0.0):
    one, two, three = split3(bias)
    sub = sub_iota(8)
    rest = jnp.where(sub < 6, other, 0.0)
    return jnp.where(sub == at, one, jnp.where(sub == at + 1, two, jnp.where(sub == at + 2, three, rest)))


def combine(parts):
    top = parts[0]
    for part in parts[1:]:
        top = jnp.maximum(top, part)
    total = jnp.exp2(parts[0] - top)
    for part in parts[1:]:
        total = total + jnp.exp2(part - top)
    return top + jnp.log(total) * LOG2E


def column_pieces(block):
    start, pieces = block * 128, []
    while start < block * 128 + 128:
        shard, offset = divmod(start, OWN_COLS)
        stop = min((shard + 1) * OWN_COLS, block * 128 + 128)
        pieces.append((shard, offset, start - block * 128, stop - block * 128))
        start = stop
    return pieces


def lse(scores):
    top = jnp.max(scores, 0, keepdims=True)
    return top + jnp.log(jnp.sum(jnp.exp2(scores - top), 0, keepdims=True)) * LOG2E


def kernel(
    src_hbm, tgt_hbm, pot_hbm, slw_hbm, tlw_hbm,
    out_ref,
    src_v, tgt_v, pot_v, slw_v, tlw_v,
    pad, smsg, tmsg, srecv, trecv,
    xr, yr, xt, yt, tl, tf, wh, wl, ya, held, peak, scr,
    slw, tlw, lpart, lsend, lrecv, csend, crecv, gsend, grecv, msend, mrecv, lall, gall,
    in_sem, s_send, s_recv, t_send, t_recv, l_send, l_recv, g_send, g_recv, m_send, m_recv, c_send, c_recv,
):
    me_t = lax.axis_index("tgt")
    me_s = lax.axis_index("src")
    me_y, me_x = me_t // 4, lax.rem(me_t, 4)
    me_z, me_c = me_s // 2, lax.rem(me_s, 2)

    def at_t(offset):
        return lax.rem(me_y + offset[0], 4) * 4 + lax.rem(me_x + offset[1], 4)

    def at_s(offset):
        return lax.rem(me_z + offset[0], 8) * 2 + lax.rem(me_c + offset[1], 2)

    barrier = pltpu.get_barrier_semaphore()
    for offset in TGT_PEERS:
        pl.semaphore_signal(barrier, inc=1, device_id={"tgt": at_t(offset)}, device_id_type=MESH)
    for offset in [(z, 0) for z in Z_PEERS] + [(0, 1)]:
        pl.semaphore_signal(barrier, inc=1, device_id={"src": at_s(offset)}, device_id_type=MESH)

    inputs = [
        pltpu.make_async_copy(a, b, in_sem.at[n])
        for n, (a, b) in enumerate(
            ((src_hbm, src_v), (slw_hbm, slw_v), (tgt_hbm, tgt_v), (pot_hbm, pot_v), (tlw_hbm, tlw_v))
        )
    ]
    for copy in inputs:
        copy.start()
    pad[...] = jnp.zeros_like(pad)
    tmsg[...] = jnp.zeros_like(tmsg)
    low = lane_iota(16) < 64
    for copy in inputs:
        copy.wait()

    pad[0:DIM, 0:OWN_ROWS] = src_v[...]
    pad[DIM : DIM + 1, 0:OWN_ROWS] = slw_v[...] * LOG2E
    own = pad[...]
    src_sq = jnp.sum(own[0:DIM] * own[0:DIM], 0, keepdims=True)
    smsg[0:16, :] = jnp.where(low, own[0:16], pltpu.roll(own[16:32], 64, 1))
    smsg[16:24, :] = own[32:40]
    tmsg[0:DIM, 0:OWN_COLS] = tgt_v[...]
    own_t = tmsg[0:DIM, :]
    tgt_sq = jnp.sum(own_t * own_t, 0, keepdims=True)
    tmsg[DIM : DIM + 1, 0:OWN_COLS] = (
        SCALE * (pot_v[...] - tgt_sq[:, 0:OWN_COLS]) + LOG2E * tlw_v[...]
    )
    tmsg[DIM + 1 : DIM + 2, 0:OWN_COLS] = LOG2E * tlw_v[...]

    pl.semaphore_wait(barrier, len(TGT_PEERS) + len(Z_PEERS) + 1)
    sent = []

    def to_t(offset, src, dst, send, recv):
        copy = pltpu.make_async_remote_copy(
            src_ref=src, dst_ref=dst, send_sem=send, recv_sem=recv.at[me_t],
            device_id={"tgt": at_t(offset)}, device_id_type=MESH,
        )
        copy.start()
        sent.append(copy)

    def to_s(offset, slot, src, dst, send, recv):
        copy = pltpu.make_async_remote_copy(
            src_ref=src, dst_ref=dst, send_sem=send, recv_sem=recv.at[slot],
            device_id={"src": at_s(offset)}, device_id_type=MESH,
        )
        copy.start()
        sent.append(copy)

    def arrive(dst, sem):
        pltpu.make_async_copy(dst, dst, sem).wait()

    tgt_own = tmsg.at[0:TGT_LINES]
    for n, z in enumerate(Z_PEERS):
        to_s((z, 0), 8 - z, tgt_own, trecv.at[0, 8 - z, 0:TGT_LINES], t_send.at[n], t_recv)
    src_own = smsg.at[0:SRC_LINES]
    for n, offset in enumerate(TGT_PEERS):
        to_t(offset, src_own, srecv.at[me_t, 0:SRC_LINES], s_send.at[n], s_recv)
    srecv[me_t] = smsg[...]
    trecv[0, 0] = tmsg[...]
    ones16 = jnp.where(sub_iota(16) < 3, 1.0, 0.0).astype(BF16)
    zeros48 = jnp.zeros((48, 128), BF16)
    zeros56 = jnp.zeros((56, 128), F32)

    def operand(n):
        tops_t, tails_t = [], []
        for z in (2 * n, 2 * n + 1):
            block = trecv[z // 8, z % 8]
            y1, y2, y3 = split3(block[0:DIM])
            tops_t.append(jnp.transpose(jnp.concatenate([y1, y2, y1, y2], 0))[0:OWN_COLS])
            tail = jnp.concatenate([y3, y1, bias_rows(block[DIM : DIM + 1]), zeros56], 0)
            tails_t.append(jnp.transpose(tail)[0:OWN_COLS])
        ya[n, :, 0:128] = jnp.concatenate(tops_t, 0).astype(BF16)
        ya[n, :, 128:256] = jnp.concatenate(tails_t, 0).astype(BF16)

    def first(n):
        scores = dot(ya[n], xr[...])
        held[n % 2] = scores
        peak[n % 2] = jnp.max(scores, 0, keepdims=True)

    def second(n):
        top = peak[n % 2]
        part = top + jnp.log(jnp.sum(jnp.exp2(held[n % 2] - top), 0, keepdims=True)) * LOG2E
        for p in range(8):
            lpart[n, p : p + 1, :] = part[:, 128 * p : 128 * p + 128]

    for z in reversed(Z_PEERS):
        arrive(trecv.at[0, 8 - z, 0:TGT_LINES], t_recv.at[8 - z])
    to_s((0, 1), 8, trecv.at[0, :, 0:TGT_LINES], trecv.at[1, :, 0:TGT_LINES], t_send.at[7], t_recv)
    operand(0)

    for offset in reversed(TGT_PEERS):
        slot = at_t(offset)
        arrive(srecv.at[slot, 0:SRC_LINES], s_recv.at[slot])
    for p in range(8):
        a, b = srecv[2 * p], srecv[2 * p + 1]
        one = jnp.where(low, a[0:16], pltpu.roll(b[0:16], 64, 1))
        two = jnp.where(low, pltpu.roll(a[0:16], 64, 1), b[0:16])
        x1, x2, x3 = split3(jnp.concatenate([one, two], 0) * (2.0 * SCALE))
        at = slice(128 * p, 128 * p + 128)
        slw[p : p + 1, :] = jnp.where(low[0:1], a[16:17], pltpu.roll(b[16:24], 64, 1)[0:1])
        xr[0:128, at] = jnp.concatenate([x1, x1, x2, x2], 0).astype(BF16)
        xr[128:192, at] = jnp.concatenate([x1, x3], 0).astype(BF16)
        xr[192:208, at] = ones16
        xr[208:256, at] = zeros48
    first(0)
    for n in range(1, 4):
        operand(n)
        first(n)
        second(n - 1)
    arrive(trecv.at[1, :, 0:TGT_LINES], t_recv.at[8])
    for n in range(4, 8):
        operand(n)
        first(n)
        second(n - 1)
    second(7)
    lsend[...] = combine([lpart[n] for n in range(8)])
    for n, offset in enumerate(TGT_PEERS):
        to_t(offset, lsend, lrecv.at[me_t], l_send.at[n], l_recv)
    lrecv[me_t] = lsend[...]

    for p in range(8):
        at = slice(128 * p, 128 * p + 128)
        xt[at, 0:128] = jnp.transpose(xr[0:128, at].astype(F32)).astype(BF16)
    for q in range(13):
        at = slice(128 * q, 128 * q + 128)
        lane = lane_iota(40)
        block = None
        for shard, offset, start, stop in column_pieces(q):
            piece = trecv[lax.rem(shard + me_c, 2), lax.rem(shard // 2 + 8 - me_z, 8)]
            shift = (start - offset) % 128
            if shift:
                piece = pltpu.roll(piece, shift, 1)
            block = piece if block is None else jnp.where(lane >= start, piece, block)
        y1, y2, y3 = split3(block[0:DIM])
        tlw[q : q + 1, :] = block[DIM + 1 : DIM + 2]
        yr[0:128, at] = jnp.concatenate([y1, y2, y1, y2], 0).astype(BF16)
        yr[128:192, at] = jnp.concatenate([y3, y1], 0).astype(BF16)
        yr[192:208, at] = ones16
        yr[208:256, at] = zeros48
        yt[at, 0:128] = jnp.transpose(jnp.concatenate([y1, y2, y1, y2], 0)).astype(BF16)
        tf[:, at] = block[0:DIM]

    for offset in reversed(TGT_PEERS):
        slot = at_t(offset)
        arrive(lrecv.at[slot], l_recv.at[slot])
    row_lse = combine([lrecv[k] for k in range(GROUP)])
    lall[...] = row_lse
    for p in range(8):
        at = slice(128 * p, 128 * p + 128)
        bias = slw[p : p + 1, :] - row_lse[p : p + 1, :]
        tail = jnp.concatenate([xr[128:192, at].astype(F32), bias_rows(bias), zeros56], 0)
        xt[at, 128:256] = jnp.transpose(tail).astype(BF16)
        both = jnp.concatenate([bias_rows(bias, 3, 1.0), jnp.zeros((8, 128), F32)], 0)
        xr[192:208, at] = both.astype(BF16)

    def first(n):
        width = min(256, COLS - 256 * n)
        scores = dot(xt[...], yr[:, 256 * n : 256 * n + width])
        scr[n % 2, 0:ROWS, 0:width] = scores
        peak[n % 2, :, 0:width] = jnp.max(scores, 0, keepdims=True)

    def second(n):
        width = min(256, COLS - 256 * n)
        top = peak[n % 2, :, 0:width]
        part = top + jnp.log(
            jnp.sum(jnp.exp2(scr[n % 2, 0:ROWS, 0:width] - top), 0, keepdims=True)
        ) * LOG2E
        for h in range(width // 128):
            csend[2 * n + h : 2 * n + h + 1, :] = part[:, 128 * h : 128 * h + 128]

    for n in range(8):
        if n < 7:
            first(n)
        if n > 0:
            second(n - 1)
    there = crecv.at[0:13]
    copy = pltpu.make_async_remote_copy(
        src_ref=csend.at[0:13], dst_ref=there, send_sem=c_send.at[0], recv_sem=c_recv.at[0],
        device_id={"src": at_s((0, 1))}, device_id_type=MESH,
    )
    copy.start()
    sent.append(copy)
    for q in range(13):
        at = slice(128 * q, 128 * q + 128)
        bias = tlw[q : q + 1, :] - csend[q : q + 1, :] - TOP_LOGW
        tail = jnp.concatenate([yr[128:192, at].astype(F32), bias_rows(bias, 0, 1.0), zeros56], 0)
        yt[at, 128:256] = jnp.transpose(tail).astype(BF16)
    arrive(there, c_recv.at[0])
    gsend[...] = combine([csend[...], crecv[...]])
    for n, z in enumerate(Z_PEERS):
        to_s((z, 0), me_z, gsend.at[0:13], grecv.at[me_z, 0:13], g_send.at[n], g_recv)
    grecv[me_z] = gsend[...]

    orders = (2, 1, 3, 0)
    for n, order in enumerate(orders):
        columns = pl.ds(pl.multiple_of(lax.rem(me_y + order, 4) * 256, 256), 256)
        for base, stop in ((0, 512), (512, 1024), (1024, 1664)):
            weights = jnp.exp2(dot(yt[base:stop, :], xr[:, columns]))
            high = weights.astype(BF16)
            wh[n, base:stop, :] = high
            wl[n, base:stop, :] = (weights - high.astype(F32)).astype(BF16)

    row = lall[pl.ds(me_y * 2 + me_x // 2, 1), :]
    row = jnp.where(lax.rem(me_t, 2) == 1, pltpu.roll(row, 64, 1), row)
    out_ref[32:33, :] = src_sq - (EPSILON / LOG2E) * row

    for z in reversed(Z_PEERS):
        slot = lax.rem(me_z + z, 8)
        arrive(grecv.at[slot, 0:13], g_recv.at[slot])
    col_lse = combine([grecv[k] for k in range(8)])
    gall[...] = col_lse
    factor = jnp.exp2(csend[...] - col_lse)
    for q in range(13):
        at = slice(128 * q, 128 * q + 128)
        scale = factor[q : q + 1, :]
        whole = tf[:, at] * scale
        one = whole.astype(BF16)
        scale_one = scale.astype(BF16).astype(F32)
        sub = sub_iota(16)
        line = jnp.where(sub == 0, scale_one, jnp.where(sub == 1, scale - scale_one, 0.0))
        tl[0:32, at] = one
        tl[32:48, at] = line.astype(BF16)
        tl[48:80, at] = (whole - one.astype(F32)).astype(BF16)
    def gather_moments(n):
        tile = lax.rem(me_y + orders[n], 4)
        main = dot(tl[...], wh[n])
        rest = dot(tl[0:48, :], wl[n])
        coords = main[0:32] + main[48:80] + rest[0:32]
        norms = main[32:40] + rest[32:40]
        norms = norms + pltpu.roll(norms, 7, 0)
        for u in range(4):
            lanes = slice(128 * (u // 2), 128 * (u // 2) + 128)
            one, two, three = coords[0:16, lanes], coords[16:32, lanes], norms[:, lanes]
            if u % 2 == 0:
                two = pltpu.roll(two, 64, 1)
            else:
                one, three = pltpu.roll(one, 64, 1), pltpu.roll(three, 64, 1)
            msend[tile * 4 + u, 0:16, :] = jnp.where(low, one, two)
            msend[tile * 4 + u, 16:24, :] = three

    for group in ((0, 1), (2, 3)):
        for n in group:
            gather_moments(n)
        for n in group:
            order = orders[n]
            tile = lax.rem(me_y + order, 4)
            for x in range(0 if order else 1, 4):
                slot = tile * 4 + lax.rem(me_x + x, 4)
                to_t((order, x), msend.at[slot, 0:SRC_LINES], mrecv.at[me_t, 0:SRC_LINES],
                     m_send.at[order * 4 + x], m_recv)
    mrecv[me_t] = msend[me_t]

    start = me_s * OWN_COLS
    line, offset = start // 128, lax.rem(start, 128)
    here = pltpu.roll(gall[pl.ds(line, 1), :], 128 - offset, 1)
    after = pltpu.roll(gall[pl.ds(line + 1, 1), :], 128 - offset, 1)
    col = jnp.where(lane_iota(1) < 128 - offset, here, after)
    out_ref[33:34, :] = tgt_sq - (EPSILON / LOG2E) * col
    out_ref[34:40, :] = jnp.zeros((6, 128), F32)

    for offset in reversed(TGT_PEERS):
        slot = at_t(offset)
        arrive(mrecv.at[slot, 0:SRC_LINES], m_recv.at[slot])
    acc, norm = mrecv[0, 0:16, :], mrecv[0, 16:17, :]
    for k in range(1, GROUP):
        acc = acc + mrecv[k, 0:16, :]
        norm = norm + mrecv[k, 16:17, :]
    ratio = acc / jnp.where(low[0:1], norm, pltpu.roll(norm, 64, 1))
    out_ref[0:16, :] = ratio
    out_ref[16:32, :] = pltpu.roll(ratio, 64, 1)
    for copy in sent:
        copy.wait_send()


def deliver(out_ref, f_ref, g_ref, p_ref):
    f_ref[...] = out_ref[32:33, 0:OWN_ROWS]
    g_ref[...] = out_ref[33:34, 0:OWN_COLS]
    p_ref[...] = out_ref[0:DIM, 0:OWN_ROWS]


def body(source, target, target_pot, source_logw, target_logw):
    vmem = pl.BlockSpec(memory_space=pltpu.VMEM)
    out = pl.pallas_call(
        kernel,
        out_shape=jax.ShapeDtypeStruct((40, 128), F32),
        in_specs=[pl.BlockSpec(memory_space=pl.ANY)] * 5,
        out_specs=vmem,
        scratch_shapes=[
            pltpu.VMEM((DIM, OWN_ROWS), F32),
            pltpu.VMEM((DIM, OWN_COLS), F32),
            pltpu.VMEM((1, OWN_COLS), F32),
            pltpu.VMEM((1, OWN_ROWS), F32),
            pltpu.VMEM((1, OWN_COLS), F32),
            pltpu.VMEM((40, 128), F32),
            pltpu.VMEM((24, 128), F32),
            pltpu.VMEM((40, 128), F32),
            pltpu.VMEM((GROUP, 24, 128), F32),
            pltpu.VMEM((2, 8, 40, 128), F32),
            pltpu.VMEM((256, ROWS), BF16),
            pltpu.VMEM((256, COLS), BF16),
            pltpu.VMEM((ROWS, 256), BF16),
            pltpu.VMEM((COLS, 256), BF16),
            pltpu.VMEM((80, COLS), BF16),
            pltpu.VMEM((DIM, COLS), F32),
            pltpu.VMEM((4, COLS, 256), BF16),
            pltpu.VMEM((4, COLS, 256), BF16),
            pltpu.VMEM((8, 2 * OWN_COLS, 256), BF16),
            pltpu.VMEM((2, 2 * OWN_COLS, ROWS), F32),
            pltpu.VMEM((2, 1, ROWS), F32),
            pltpu.VMEM((2, ROWS, 256), F32),
            pltpu.VMEM((8, 128), F32),
            pltpu.VMEM((16, 128), F32),
            pltpu.VMEM((8, 8, 128), F32),
            pltpu.VMEM((8, 128), F32),
            pltpu.VMEM((GROUP, 8, 128), F32),
            pltpu.VMEM((16, 128), F32),
            pltpu.VMEM((16, 128), F32),
            pltpu.VMEM((16, 128), F32),
            pltpu.VMEM((8, 16, 128), F32),
            pltpu.VMEM((GROUP, 24, 128), F32),
            pltpu.VMEM((GROUP, 24, 128), F32),
            pltpu.VMEM((8, 128), F32),
            pltpu.VMEM((16, 128), F32),
            pltpu.SemaphoreType.DMA((5,)),
        ]
        + [pltpu.SemaphoreType.DMA((GROUP,))] * 6
        + [pltpu.SemaphoreType.DMA((GROUP,))] * 4
        + [pltpu.SemaphoreType.DMA((1,))] * 2,
        compiler_params=pltpu.CompilerParams(
            collective_id=0, has_side_effects=True, vmem_limit_bytes=60 * 1024 * 1024
        ),
    )(
        source,
        target,
        target_pot.reshape(1, OWN_COLS),
        source_logw.reshape(1, OWN_ROWS),
        target_logw.reshape(1, OWN_COLS),
    )
    f_new, g_new, projection = pl.pallas_call(
        deliver,
        out_shape=(
            jax.ShapeDtypeStruct((1, OWN_ROWS), F32),
            jax.ShapeDtypeStruct((1, OWN_COLS), F32),
            jax.ShapeDtypeStruct((DIM, OWN_ROWS), F32),
        ),
        in_specs=[vmem],
        out_specs=(vmem,) * 3,
    )(out)
    return f_new.reshape(OWN_ROWS), g_new.reshape(OWN_COLS), projection


def solution(mesh):
    return jax.shard_map(
        body,
        mesh=mesh,
        in_specs=(
            P(None, ("src", "tgt")),
            P(None, ("tgt", "src")),
            P(("tgt", "src")),
            P(("src", "tgt")),
            P(("tgt", "src")),
        ),
        out_specs=(P(("src", "tgt")), P(("tgt", "src")), P(None, ("src", "tgt"))),
        check_vma=False,
    )
```

```python
import math

import jax
import jax.numpy as jnp
from jax import lax
from jax.experimental import pallas as pl
from jax.experimental.pallas import tpu as pltpu
from jax.sharding import PartitionSpec as P

EPSILON = 0.05
LOG2E = 1.0 / math.log(2.0)
SCALE = LOG2E / EPSILON
TOP_LOGW = -9.0 * LOG2E
F32 = jnp.float32
BF16 = jnp.bfloat16
MESH = pl.DeviceIdType.MESH
GROUP = 16
ROWS = 1024
COLS = 1664
OWN_ROWS = 64
OWN_COLS = 104
DIM = 32
SRC_LINES = 17
TGT_LINES = 34


def ring(d, n):
    return min(d, n - d)


TGT_PEERS = sorted(
    [(y, x) for y in range(4) for x in range(4) if y or x],
    key=lambda o: -(ring(o[0], 4) + ring(o[1], 4)),
)
Z_PEERS = (4, 3, 5, 2, 6, 1, 7)


def dot(a, b):
    return lax.dot_general(a, b, (((1,), (0,)), ((), ())), preferred_element_type=F32)


def split3(x):
    one = x.astype(BF16).astype(F32)
    rest = x - one
    two = rest.astype(BF16).astype(F32)
    return one, two, rest - two


def lane_iota(rows):
    return lax.broadcasted_iota(jnp.int32, (rows, 128), 1)


def sub_iota(rows):
    return lax.broadcasted_iota(jnp.int32, (rows, 128), 0)


def bias_rows(bias, at=0, other=0.0):
    one, two, three = split3(bias)
    sub = sub_iota(8)
    rest = jnp.where(sub < 6, other, 0.0)
    return jnp.where(sub == at, one, jnp.where(sub == at + 1, two, jnp.where(sub == at + 2, three, rest)))


def combine(parts):
    top = parts[0]
    for part in parts[1:]:
        top = jnp.maximum(top, part)
    total = jnp.exp2(parts[0] - top)
    for part in parts[1:]:
        total = total + jnp.exp2(part - top)
    return top + jnp.log(total) * LOG2E


def column_pieces(block):
    start, pieces = block * 128, []
    while start < block * 128 + 128:
        shard, offset = divmod(start, OWN_COLS)
        stop = min((shard + 1) * OWN_COLS, block * 128 + 128)
        pieces.append((shard, offset, start - block * 128, stop - block * 128))
        start = stop
    return pieces


def lse(scores):
    top = jnp.max(scores, 0, keepdims=True)
    return top + jnp.log(jnp.sum(jnp.exp2(scores - top), 0, keepdims=True)) * LOG2E


def kernel(
    src_hbm, tgt_hbm, pot_hbm, slw_hbm, tlw_hbm,
    out_ref,
    src_v, tgt_v, pot_v, slw_v, tlw_v,
    pad, smsg, tmsg, srecv, trecv,
    xr, yr, xt, yt, tl, tf, wh, wl, ya, held, peak, scr,
    slw, tlw, lpart, lsend, lrecv, cpart, csend, crecv, gsend, grecv, msend, mrecv, lall, gall,
    in_sem, s_send, s_recv, t_send, t_recv, l_send, l_recv, g_send, g_recv, m_send, m_recv, c_send, c_recv,
):
    me_t = lax.axis_index("tgt")
    me_s = lax.axis_index("src")
    me_y, me_x = me_t // 4, lax.rem(me_t, 4)
    me_z, me_c = me_s // 2, lax.rem(me_s, 2)

    def at_t(offset):
        return lax.rem(me_y + offset[0], 4) * 4 + lax.rem(me_x + offset[1], 4)

    def at_s(offset):
        return lax.rem(me_z + offset[0], 8) * 2 + lax.rem(me_c + offset[1], 2)

    barrier = pltpu.get_barrier_semaphore()
    for offset in [(z, 0) for z in Z_PEERS] + [(0, 1)]:
        pl.semaphore_signal(barrier, inc=1, device_id={"src": at_s(offset)}, device_id_type=MESH)
    for offset in TGT_PEERS:
        pl.semaphore_signal(barrier, inc=1, device_id={"tgt": at_t(offset)}, device_id_type=MESH)

    inputs = [
        pltpu.make_async_copy(a, b, in_sem.at[n])
        for n, (a, b) in enumerate(
            ((src_hbm, src_v), (slw_hbm, slw_v), (tgt_hbm, tgt_v), (pot_hbm, pot_v), (tlw_hbm, tlw_v))
        )
    ]
    for copy in inputs:
        copy.start()
    pad[...] = jnp.zeros_like(pad)
    tmsg[...] = jnp.zeros_like(tmsg)
    low = lane_iota(16) < 64
    for copy in inputs:
        copy.wait()

    pad[0:DIM, 0:OWN_ROWS] = src_v[...]
    pad[DIM : DIM + 1, 0:OWN_ROWS] = slw_v[...] * LOG2E
    own = pad[...]
    src_sq = jnp.sum(own[0:DIM] * own[0:DIM], 0, keepdims=True)
    smsg[0:16, :] = jnp.where(low, own[0:16], pltpu.roll(own[16:32], 64, 1))
    smsg[16:24, :] = own[32:40]
    tmsg[0:DIM, 0:OWN_COLS] = tgt_v[...]
    own_t = tmsg[0:DIM, :]
    tgt_sq = jnp.sum(own_t * own_t, 0, keepdims=True)
    tmsg[DIM : DIM + 1, 0:OWN_COLS] = (
        SCALE * (pot_v[...] - tgt_sq[:, 0:OWN_COLS]) + LOG2E * tlw_v[...]
    )
    tmsg[DIM + 1 : DIM + 2, 0:OWN_COLS] = LOG2E * tlw_v[...]

    pl.semaphore_wait(barrier, len(TGT_PEERS) + len(Z_PEERS) + 1)
    sent = []

    def to_t(offset, src, dst, send, recv):
        copy = pltpu.make_async_remote_copy(
            src_ref=src, dst_ref=dst, send_sem=send, recv_sem=recv.at[me_t],
            device_id={"tgt": at_t(offset)}, device_id_type=MESH,
        )
        copy.start()
        sent.append(copy)

    def to_s(offset, slot, src, dst, send, recv):
        copy = pltpu.make_async_remote_copy(
            src_ref=src, dst_ref=dst, send_sem=send, recv_sem=recv.at[slot],
            device_id={"src": at_s(offset)}, device_id_type=MESH,
        )
        copy.start()
        sent.append(copy)

    def arrive(dst, sem):
        pltpu.make_async_copy(dst, dst, sem).wait()

    tgt_own = tmsg.at[0:TGT_LINES]
    for n, z in enumerate(Z_PEERS):
        to_s((z, 0), 8 - z, tgt_own, trecv.at[0, 8 - z, 0:TGT_LINES], t_send.at[n], t_recv)
    src_own = smsg.at[0:SRC_LINES]
    for n, offset in enumerate(TGT_PEERS):
        to_t(offset, src_own, srecv.at[me_t, 0:SRC_LINES], s_send.at[n], s_recv)
    srecv[me_t] = smsg[...]
    trecv[0, 0] = tmsg[...]
    ones16 = jnp.where(sub_iota(16) < 3, 1.0, 0.0).astype(BF16)
    zeros48 = jnp.zeros((48, 128), BF16)
    zeros56 = jnp.zeros((56, 128), F32)

    def operand(n):
        tops_t, tails_t = [], []
        for z in (2 * n, 2 * n + 1):
            block = trecv[z // 8, z % 8]
            y1, y2, y3 = split3(block[0:DIM])
            tops_t.append(jnp.transpose(jnp.concatenate([y1, y2, y1, y2], 0))[0:OWN_COLS])
            tail = jnp.concatenate([y3, y1, bias_rows(block[DIM : DIM + 1]), zeros56], 0)
            tails_t.append(jnp.transpose(tail)[0:OWN_COLS])
        ya[n, :, 0:128] = jnp.concatenate(tops_t, 0).astype(BF16)
        ya[n, :, 128:256] = jnp.concatenate(tails_t, 0).astype(BF16)

    def second(n):
        for t in range(4):
            part = lse(dot(ya[n], xr[:, 256 * t : 256 * t + 256]))
            lpart[n, 2 * t : 2 * t + 1, :] = part[:, 0:128]
            lpart[n, 2 * t + 1 : 2 * t + 2, :] = part[:, 128:256]

    for z in reversed(Z_PEERS):
        arrive(trecv.at[0, 8 - z, 0:TGT_LINES], t_recv.at[8 - z])
    to_s((0, 1), 8, trecv.at[0, :, 0:TGT_LINES], trecv.at[1, :, 0:TGT_LINES], t_send.at[7], t_recv)
    operand(0)

    for offset in reversed(TGT_PEERS):
        slot = at_t(offset)
        arrive(srecv.at[slot, 0:SRC_LINES], s_recv.at[slot])
    for p in range(8):
        a, b = srecv[2 * p], srecv[2 * p + 1]
        one = jnp.where(low, a[0:16], pltpu.roll(b[0:16], 64, 1))
        two = jnp.where(low, pltpu.roll(a[0:16], 64, 1), b[0:16])
        x1, x2, x3 = split3(jnp.concatenate([one, two], 0) * (2.0 * SCALE))
        at = slice(128 * p, 128 * p + 128)
        slw[p : p + 1, :] = jnp.where(low[0:1], a[16:17], pltpu.roll(b[16:24], 64, 1)[0:1])
        xr[0:128, at] = jnp.concatenate([x1, x1, x2, x2], 0).astype(BF16)
        xr[128:192, at] = jnp.concatenate([x1, x3], 0).astype(BF16)
        xr[192:208, at] = ones16
        xr[208:256, at] = zeros48
    second(0)
    for n in range(1, 4):
        operand(n)
        second(n)
    arrive(trecv.at[1, :, 0:TGT_LINES], t_recv.at[8])
    for n in range(4, 8):
        operand(n)
        second(n)
    lsend[...] = combine([lpart[n] for n in range(8)])
    for n, offset in enumerate(TGT_PEERS):
        to_t(offset, lsend, lrecv.at[me_t], l_send.at[n], l_recv)
    lrecv[me_t] = lsend[...]

    for p in range(8):
        at = slice(128 * p, 128 * p + 128)
        xt[at, 0:128] = jnp.transpose(xr[0:128, at].astype(F32)).astype(BF16)
    for q in range(13):
        at = slice(128 * q, 128 * q + 128)
        lane = lane_iota(40)
        block = None
        for shard, offset, start, stop in column_pieces(q):
            piece = trecv[lax.rem(shard + me_c, 2), lax.rem(shard // 2 + 8 - me_z, 8)]
            shift = (start - offset) % 128
            if shift:
                piece = pltpu.roll(piece, shift, 1)
            block = piece if block is None else jnp.where(lane >= start, piece, block)
        y1, y2, y3 = split3(block[0:DIM])
        tlw[q : q + 1, :] = block[DIM + 1 : DIM + 2]
        yr[0:128, at] = jnp.concatenate([y1, y2, y1, y2], 0).astype(BF16)
        yr[128:192, at] = jnp.concatenate([y3, y1], 0).astype(BF16)
        yr[192:208, at] = ones16
        yr[208:256, at] = zeros48
        yt[at, 0:128] = jnp.transpose(jnp.concatenate([y1, y2, y1, y2], 0)).astype(BF16)
        tf[:, at] = block[0:DIM]

    for offset in reversed(TGT_PEERS):
        slot = at_t(offset)
        arrive(lrecv.at[slot], l_recv.at[slot])
    row_lse = combine([lrecv[k] for k in range(GROUP)])
    lall[...] = row_lse
    for p in range(8):
        at = slice(128 * p, 128 * p + 128)
        bias = slw[p : p + 1, :] - row_lse[p : p + 1, :]
        tail = jnp.concatenate([xr[128:192, at].astype(F32), bias_rows(bias), zeros56], 0)
        xt[at, 128:256] = jnp.transpose(tail).astype(BF16)
        both = jnp.concatenate([bias_rows(bias, 3, 1.0), jnp.zeros((8, 128), F32)], 0)
        xr[192:208, at] = both.astype(BF16)

    def block_rows(r, carry):
        rows = xt[pl.ds(pl.multiple_of(r * 256, 256), 256), :]
        for n in range(7):
            width = min(256, COLS - 256 * n)
            part = lse(dot(rows, yr[:, 256 * n : 256 * n + width]))
            for h in range(width // 128):
                cpart[r, 2 * n + h : 2 * n + h + 1, :] = part[:, 128 * h : 128 * h + 128]
        return carry

    for r in range(4):
        block_rows(r, 0)
    csend[...] = combine([cpart[r] for r in range(4)])
    there = crecv.at[0:13]
    copy = pltpu.make_async_remote_copy(
        src_ref=csend.at[0:13], dst_ref=there, send_sem=c_send.at[0], recv_sem=c_recv.at[0],
        device_id={"src": at_s((0, 1))}, device_id_type=MESH,
    )
    copy.start()
    sent.append(copy)
    for q in range(13):
        at = slice(128 * q, 128 * q + 128)
        bias = tlw[q : q + 1, :] - csend[q : q + 1, :] - TOP_LOGW
        tail = jnp.concatenate([yr[128:192, at].astype(F32), bias_rows(bias, 0, 1.0), zeros56], 0)
        yt[at, 128:256] = jnp.transpose(tail).astype(BF16)
    arrive(there, c_recv.at[0])
    gsend[...] = combine([csend[...], crecv[...]])
    for n, z in enumerate(Z_PEERS):
        to_s((z, 0), me_z, gsend.at[0:13], grecv.at[me_z, 0:13], g_send.at[n], g_recv)
    grecv[me_z] = gsend[...]

    orders = (2, 1, 3, 0)
    for n, order in enumerate(orders):
        columns = pl.ds(pl.multiple_of(lax.rem(me_y + order, 4) * 256, 256), 256)
        for base, stop in ((0, 512), (512, 1024), (1024, 1664)):
            weights = jnp.exp2(dot(yt[base:stop, :], xr[:, columns]))
            high = weights.astype(BF16)
            wh[n, base:stop, :] = high
            wl[n, base:stop, :] = (weights - high.astype(F32)).astype(BF16)

    row = lall[pl.ds(me_y * 2 + me_x // 2, 1), :]
    row = jnp.where(lax.rem(me_t, 2) == 1, pltpu.roll(row, 64, 1), row)
    out_ref[32:33, :] = src_sq - (EPSILON / LOG2E) * row

    for z in reversed(Z_PEERS):
        slot = lax.rem(me_z + z, 8)
        arrive(grecv.at[slot, 0:13], g_recv.at[slot])
    col_lse = combine([grecv[k] for k in range(8)])
    gall[...] = col_lse
    factor = jnp.exp2(csend[...] - col_lse)
    for q in range(13):
        at = slice(128 * q, 128 * q + 128)
        scale = factor[q : q + 1, :]
        whole = tf[:, at] * scale
        one = whole.astype(BF16)
        scale_one = scale.astype(BF16).astype(F32)
        sub = sub_iota(16)
        line = jnp.where(sub == 0, scale_one, jnp.where(sub == 1, scale - scale_one, 0.0))
        tl[0:32, at] = one
        tl[32:48, at] = line.astype(BF16)
        tl[48:80, at] = (whole - one.astype(F32)).astype(BF16)
    def gather_moments(n):
        tile = lax.rem(me_y + orders[n], 4)
        main = dot(tl[...], wh[n])
        rest = dot(tl[0:48, :], wl[n])
        coords = main[0:32] + main[48:80] + rest[0:32]
        norms = main[32:40] + rest[32:40]
        norms = norms + pltpu.roll(norms, 7, 0)
        for u in range(4):
            lanes = slice(128 * (u // 2), 128 * (u // 2) + 128)
            one, two, three = coords[0:16, lanes], coords[16:32, lanes], norms[:, lanes]
            if u % 2 == 0:
                two = pltpu.roll(two, 64, 1)
            else:
                one, three = pltpu.roll(one, 64, 1), pltpu.roll(three, 64, 1)
            msend[tile * 4 + u, 0:16, :] = jnp.where(low, one, two)
            msend[tile * 4 + u, 16:24, :] = three

    for group in ((0, 1), (2, 3)):
        for n in group:
            gather_moments(n)
        for n in group:
            order = orders[n]
            tile = lax.rem(me_y + order, 4)
            for x in range(0 if order else 1, 4):
                slot = tile * 4 + lax.rem(me_x + x, 4)
                to_t((order, x), msend.at[slot, 0:SRC_LINES], mrecv.at[me_t, 0:SRC_LINES],
                     m_send.at[order * 4 + x], m_recv)
    mrecv[me_t] = msend[me_t]

    start = me_s * OWN_COLS
    line, offset = start // 128, lax.rem(start, 128)
    here = pltpu.roll(gall[pl.ds(line, 1), :], 128 - offset, 1)
    after = pltpu.roll(gall[pl.ds(line + 1, 1), :], 128 - offset, 1)
    col = jnp.where(lane_iota(1) < 128 - offset, here, after)
    out_ref[33:34, :] = tgt_sq - (EPSILON / LOG2E) * col
    out_ref[34:40, :] = jnp.zeros((6, 128), F32)

    for offset in reversed(TGT_PEERS):
        slot = at_t(offset)
        arrive(mrecv.at[slot, 0:SRC_LINES], m_recv.at[slot])
    acc, norm = mrecv[0, 0:16, :], mrecv[0, 16:17, :]
    for k in range(1, GROUP):
        acc = acc + mrecv[k, 0:16, :]
        norm = norm + mrecv[k, 16:17, :]
    ratio = acc / jnp.where(low[0:1], norm, pltpu.roll(norm, 64, 1))
    out_ref[0:16, :] = ratio
    out_ref[16:32, :] = pltpu.roll(ratio, 64, 1)
    for copy in sent:
        copy.wait_send()


def deliver(out_ref, f_ref, g_ref, p_ref):
    f_ref[...] = out_ref[32:33, 0:OWN_ROWS]
    g_ref[...] = out_ref[33:34, 0:OWN_COLS]
    p_ref[...] = out_ref[0:DIM, 0:OWN_ROWS]


def body(source, target, target_pot, source_logw, target_logw):
    vmem = pl.BlockSpec(memory_space=pltpu.VMEM)
    out = pl.pallas_call(
        kernel,
        out_shape=pltpu.VMEM((40, 128), F32),
        in_specs=[pl.BlockSpec(memory_space=pl.ANY)] * 5,
        out_specs=vmem,
        scratch_shapes=[
            pltpu.VMEM((DIM, OWN_ROWS), F32),
            pltpu.VMEM((DIM, OWN_COLS), F32),
            pltpu.VMEM((1, OWN_COLS), F32),
            pltpu.VMEM((1, OWN_ROWS), F32),
            pltpu.VMEM((1, OWN_COLS), F32),
            pltpu.VMEM((40, 128), F32),
            pltpu.VMEM((24, 128), F32),
            pltpu.VMEM((40, 128), F32),
            pltpu.VMEM((GROUP, 24, 128), F32),
            pltpu.VMEM((2, 8, 40, 128), F32),
            pltpu.VMEM((256, ROWS), BF16),
            pltpu.VMEM((256, COLS), BF16),
            pltpu.VMEM((ROWS, 256), BF16),
            pltpu.VMEM((COLS, 256), BF16),
            pltpu.VMEM((80, COLS), BF16),
            pltpu.VMEM((DIM, COLS), F32),
            pltpu.VMEM((4, COLS, 256), BF16),
            pltpu.VMEM((4, COLS, 256), BF16),
            pltpu.VMEM((8, 2 * OWN_COLS, 256), BF16),
            pltpu.VMEM((2, 2 * OWN_COLS, ROWS), F32),
            pltpu.VMEM((2, 1, ROWS), F32),
            pltpu.VMEM((2, ROWS, 256), F32),
            pltpu.VMEM((8, 128), F32),
            pltpu.VMEM((16, 128), F32),
            pltpu.VMEM((8, 8, 128), F32),
            pltpu.VMEM((8, 128), F32),
            pltpu.VMEM((GROUP, 8, 128), F32),
            pltpu.VMEM((4, 16, 128), F32),
            pltpu.VMEM((16, 128), F32),
            pltpu.VMEM((16, 128), F32),
            pltpu.VMEM((16, 128), F32),
            pltpu.VMEM((8, 16, 128), F32),
            pltpu.VMEM((GROUP, 24, 128), F32),
            pltpu.VMEM((GROUP, 24, 128), F32),
            pltpu.VMEM((8, 128), F32),
            pltpu.VMEM((16, 128), F32),
            pltpu.SemaphoreType.DMA((5,)),
        ]
        + [pltpu.SemaphoreType.DMA((GROUP,))] * 6
        + [pltpu.SemaphoreType.DMA((GROUP,))] * 4
        + [pltpu.SemaphoreType.DMA((1,))] * 2,
        compiler_params=pltpu.CompilerParams(
            collective_id=0, has_side_effects=True, vmem_limit_bytes=60 * 1024 * 1024
        ),
    )(
        source,
        target,
        target_pot.reshape(1, OWN_COLS),
        source_logw.reshape(1, OWN_ROWS),
        target_logw.reshape(1, OWN_COLS),
    )
    f_new, g_new, projection = pl.pallas_call(
        deliver,
        out_shape=(
            jax.ShapeDtypeStruct((1, OWN_ROWS), F32),
            jax.ShapeDtypeStruct((1, OWN_COLS), F32),
            jax.ShapeDtypeStruct((DIM, OWN_ROWS), F32),
        ),
        in_specs=[vmem],
        out_specs=(vmem,) * 3,
    )(pltpu.with_memory_space_constraint(out, pltpu.VMEM))
    return f_new.reshape(OWN_ROWS), g_new.reshape(OWN_COLS), projection


def solution(mesh):
    return jax.shard_map(
        body,
        mesh=mesh,
        in_specs=(
            P(None, ("src", "tgt")),
            P(None, ("tgt", "src")),
            P(("tgt", "src")),
            P(("src", "tgt")),
            P(("tgt", "src")),
        ),
        out_specs=(P(("src", "tgt")), P(("tgt", "src")), P(None, ("src", "tgt"))),
        check_vma=False,
    )
```

```python
import math

import jax
import jax.numpy as jnp
from jax import lax
from jax.experimental import pallas as pl
from jax.experimental.pallas import tpu as pltpu
from jax.sharding import PartitionSpec as P

EPSILON = 0.05
LOG2E = 1.0 / math.log(2.0)
SCALE = LOG2E / EPSILON
TOP_LOGW = -9.0 * LOG2E
F32 = jnp.float32
BF16 = jnp.bfloat16
MESH = pl.DeviceIdType.MESH
GROUP = 16
ROWS = 1024
COLS = 1664
OWN_ROWS = 64
OWN_COLS = 104
DIM = 32
SRC_LINES = 17
TGT_LINES = 34


def ring(d, n):
    return min(d, n - d)


TGT_PEERS = sorted(
    [(y, x) for y in range(4) for x in range(4) if y or x],
    key=lambda o: -(ring(o[0], 4) + ring(o[1], 4)),
)
Z_PEERS = (4, 3, 5, 2, 6, 1, 7)


def dot(a, b):
    return lax.dot_general(a, b, (((1,), (0,)), ((), ())), preferred_element_type=F32)


def split3(x):
    one = x.astype(BF16).astype(F32)
    rest = x - one
    two = rest.astype(BF16).astype(F32)
    return one, two, rest - two


def lane_iota(rows):
    return lax.broadcasted_iota(jnp.int32, (rows, 128), 1)


def sub_iota(rows):
    return lax.broadcasted_iota(jnp.int32, (rows, 128), 0)


def bias_rows(bias, at=0, other=0.0):
    one, two, three = split3(bias)
    sub = sub_iota(8)
    rest = jnp.where(sub < 6, other, 0.0)
    return jnp.where(sub == at, one, jnp.where(sub == at + 1, two, jnp.where(sub == at + 2, three, rest)))


def combine(parts):
    top = parts[0]
    for part in parts[1:]:
        top = jnp.maximum(top, part)
    total = jnp.exp2(parts[0] - top)
    for part in parts[1:]:
        total = total + jnp.exp2(part - top)
    return top + jnp.log(total) * LOG2E


def column_pieces(block):
    start, pieces = block * 128, []
    while start < block * 128 + 128:
        shard, offset = divmod(start, OWN_COLS)
        stop = min((shard + 1) * OWN_COLS, block * 128 + 128)
        pieces.append((shard, offset, start - block * 128, stop - block * 128))
        start = stop
    return pieces


def lse(scores):
    top = jnp.max(scores, 0, keepdims=True)
    return top + jnp.log(jnp.sum(jnp.exp2(scores - top), 0, keepdims=True)) * LOG2E


def kernel(
    src_hbm, tgt_hbm, pot_hbm, slw_hbm, tlw_hbm,
    out_ref,
    src_v, tgt_v, pot_v, slw_v, tlw_v,
    pad, smsg, tmsg, srecv, trecv,
    xr, yr, xt, yt, tl, tf, wh, wl, ya, held, peak, scr,
    slw, tlw, lpart, lsend, lrecv, cpart, csend, crecv, gsend, grecv, msend, mrecv, lall, gall,
    in_sem, s_send, s_recv, t_send, t_recv, l_send, l_recv, g_send, g_recv, m_send, m_recv, c_send, c_recv,
):
    me_t = lax.axis_index("tgt")
    me_s = lax.axis_index("src")
    me_y, me_x = me_t // 4, lax.rem(me_t, 4)
    me_z, me_c = me_s // 2, lax.rem(me_s, 2)

    def at_t(offset):
        return lax.rem(me_y + offset[0], 4) * 4 + lax.rem(me_x + offset[1], 4)

    def at_s(offset):
        return lax.rem(me_z + offset[0], 8) * 2 + lax.rem(me_c + offset[1], 2)

    barrier = pltpu.get_barrier_semaphore()
    for offset in [(z, 0) for z in Z_PEERS] + [(0, 1)]:
        pl.semaphore_signal(barrier, inc=1, device_id={"src": at_s(offset)}, device_id_type=MESH)
    for offset in TGT_PEERS:
        pl.semaphore_signal(barrier, inc=1, device_id={"tgt": at_t(offset)}, device_id_type=MESH)

    inputs = [
        pltpu.make_async_copy(a, b, in_sem.at[n])
        for n, (a, b) in enumerate(
            ((src_hbm, src_v), (slw_hbm, slw_v), (tgt_hbm, tgt_v), (pot_hbm, pot_v), (tlw_hbm, tlw_v))
        )
    ]
    for copy in inputs:
        copy.start()
    pad[...] = jnp.zeros_like(pad)
    tmsg[...] = jnp.zeros_like(tmsg)
    low = lane_iota(16) < 64
    for copy in inputs:
        copy.wait()

    pad[0:DIM, 0:OWN_ROWS] = src_v[...]
    pad[DIM : DIM + 1, 0:OWN_ROWS] = slw_v[...] * LOG2E
    own = pad[...]
    src_sq = jnp.sum(own[0:DIM] * own[0:DIM], 0, keepdims=True)
    smsg[0:16, :] = jnp.where(low, own[0:16], pltpu.roll(own[16:32], 64, 1))
    smsg[16:24, :] = own[32:40]
    tmsg[0:DIM, 0:OWN_COLS] = tgt_v[...]
    own_t = tmsg[0:DIM, :]
    tgt_sq = jnp.sum(own_t * own_t, 0, keepdims=True)
    tmsg[DIM : DIM + 1, 0:OWN_COLS] = (
        SCALE * (pot_v[...] - tgt_sq[:, 0:OWN_COLS]) + LOG2E * tlw_v[...]
    )
    tmsg[DIM + 1 : DIM + 2, 0:OWN_COLS] = LOG2E * tlw_v[...]

    pl.semaphore_wait(barrier, len(TGT_PEERS) + len(Z_PEERS) + 1)
    sent = []

    def to_t(offset, src, dst, send, recv):
        copy = pltpu.make_async_remote_copy(
            src_ref=src, dst_ref=dst, send_sem=send, recv_sem=recv.at[me_t],
            device_id={"tgt": at_t(offset)}, device_id_type=MESH,
        )
        copy.start()
        sent.append(copy)

    def to_s(offset, slot, src, dst, send, recv):
        copy = pltpu.make_async_remote_copy(
            src_ref=src, dst_ref=dst, send_sem=send, recv_sem=recv.at[slot],
            device_id={"src": at_s(offset)}, device_id_type=MESH,
        )
        copy.start()
        sent.append(copy)

    def arrive(dst, sem):
        pltpu.make_async_copy(dst, dst, sem).wait()

    tgt_own = tmsg.at[0:TGT_LINES]
    for n, z in enumerate(Z_PEERS):
        to_s((z, 0), 8 - z, tgt_own, trecv.at[0, 8 - z, 0:TGT_LINES], t_send.at[n], t_recv)
    src_own = smsg.at[0:SRC_LINES]
    for n, offset in enumerate(TGT_PEERS):
        to_t(offset, src_own, srecv.at[me_t, 0:SRC_LINES], s_send.at[n], s_recv)
    srecv[me_t] = smsg[...]
    trecv[0, 0] = tmsg[...]
    ones16 = jnp.where(sub_iota(16) < 3, 1.0, 0.0).astype(BF16)
    zeros48 = jnp.zeros((48, 128), BF16)
    zeros56 = jnp.zeros((56, 128), F32)

    def operand(n):
        tops_t, tails_t = [], []
        for z in (2 * n, 2 * n + 1):
            block = trecv[z // 8, z % 8]
            y1, y2, y3 = split3(block[0:DIM])
            tops_t.append(jnp.transpose(jnp.concatenate([y1, y2, y1, y2], 0))[0:OWN_COLS])
            tail = jnp.concatenate([y3, y1, bias_rows(block[DIM : DIM + 1]), zeros56], 0)
            tails_t.append(jnp.transpose(tail)[0:OWN_COLS])
        ya[n, :, 0:128] = jnp.concatenate(tops_t, 0).astype(BF16)
        ya[n, :, 128:256] = jnp.concatenate(tails_t, 0).astype(BF16)

    def second(n):
        for t in range(4):
            part = lse(dot(ya[n], xr[:, 256 * t : 256 * t + 256]))
            lpart[n, 2 * t : 2 * t + 1, :] = part[:, 0:128]
            lpart[n, 2 * t + 1 : 2 * t + 2, :] = part[:, 128:256]

    for z in reversed(Z_PEERS):
        arrive(trecv.at[0, 8 - z, 0:TGT_LINES], t_recv.at[8 - z])
    to_s((0, 1), 8, trecv.at[0, :, 0:TGT_LINES], trecv.at[1, :, 0:TGT_LINES], t_send.at[7], t_recv)
    operand(0)

    for offset in reversed(TGT_PEERS):
        slot = at_t(offset)
        arrive(srecv.at[slot, 0:SRC_LINES], s_recv.at[slot])
    for p in range(8):
        a, b = srecv[2 * p], srecv[2 * p + 1]
        one = jnp.where(low, a[0:16], pltpu.roll(b[0:16], 64, 1))
        two = jnp.where(low, pltpu.roll(a[0:16], 64, 1), b[0:16])
        x1, x2, x3 = split3(jnp.concatenate([one, two], 0) * (2.0 * SCALE))
        at = slice(128 * p, 128 * p + 128)
        slw[p : p + 1, :] = jnp.where(low[0:1], a[16:17], pltpu.roll(b[16:24], 64, 1)[0:1])
        xr[0:128, at] = jnp.concatenate([x1, x1, x2, x2], 0).astype(BF16)
        xr[128:192, at] = jnp.concatenate([x1, x3], 0).astype(BF16)
        xr[192:208, at] = ones16
        xr[208:256, at] = zeros48
    second(0)
    for n in range(1, 4):
        operand(n)
        second(n)
    arrive(trecv.at[1, :, 0:TGT_LINES], t_recv.at[8])
    for n in range(4, 8):
        operand(n)
        second(n)
    lsend[...] = combine([lpart[n] for n in range(8)])
    for n, offset in enumerate(TGT_PEERS):
        to_t(offset, lsend, lrecv.at[me_t], l_send.at[n], l_recv)
    lrecv[me_t] = lsend[...]

    for p in range(8):
        at = slice(128 * p, 128 * p + 128)
        xt[at, 0:128] = jnp.transpose(xr[0:128, at].astype(F32)).astype(BF16)
    for q in range(13):
        at = slice(128 * q, 128 * q + 128)
        lane = lane_iota(40)
        block = None
        for shard, offset, start, stop in column_pieces(q):
            piece = trecv[lax.rem(shard + me_c, 2), lax.rem(shard // 2 + 8 - me_z, 8)]
            shift = (start - offset) % 128
            if shift:
                piece = pltpu.roll(piece, shift, 1)
            block = piece if block is None else jnp.where(lane >= start, piece, block)
        y1, y2, y3 = split3(block[0:DIM])
        tlw[q : q + 1, :] = block[DIM + 1 : DIM + 2]
        yr[0:128, at] = jnp.concatenate([y1, y2, y1, y2], 0).astype(BF16)
        yr[128:192, at] = jnp.concatenate([y3, y1], 0).astype(BF16)
        yr[192:208, at] = ones16
        yr[208:256, at] = zeros48
        yt[at, 0:128] = jnp.transpose(jnp.concatenate([y1, y2, y1, y2], 0)).astype(BF16)
        tf[:, at] = block[0:DIM]

    for offset in reversed(TGT_PEERS):
        slot = at_t(offset)
        arrive(lrecv.at[slot], l_recv.at[slot])
    row_lse = combine([lrecv[k] for k in range(GROUP)])
    lall[...] = row_lse
    for p in range(8):
        at = slice(128 * p, 128 * p + 128)
        bias = slw[p : p + 1, :] - row_lse[p : p + 1, :]
        tail = jnp.concatenate([xr[128:192, at].astype(F32), bias_rows(bias), zeros56], 0)
        xt[at, 128:256] = jnp.transpose(tail).astype(BF16)
        both = jnp.concatenate([bias_rows(bias, 3, 1.0), jnp.zeros((8, 128), F32)], 0)
        xr[192:208, at] = both.astype(BF16)

    def block_rows(r, carry):
        rows = xt[pl.ds(pl.multiple_of(r * 256, 256), 256), :]
        for n in range(7):
            width = min(256, COLS - 256 * n)
            part = lse(dot(rows, yr[:, 256 * n : 256 * n + width]))
            for h in range(width // 128):
                cpart[r, 2 * n + h : 2 * n + h + 1, :] = part[:, 128 * h : 128 * h + 128]
        return carry

    for r in range(4):
        block_rows(r, 0)
    csend[...] = combine([cpart[r] for r in range(4)])
    there = crecv.at[0:13]
    copy = pltpu.make_async_remote_copy(
        src_ref=csend.at[0:13], dst_ref=there, send_sem=c_send.at[0], recv_sem=c_recv.at[0],
        device_id={"src": at_s((0, 1))}, device_id_type=MESH,
    )
    copy.start()
    sent.append(copy)
    for q in range(13):
        at = slice(128 * q, 128 * q + 128)
        bias = tlw[q : q + 1, :] - csend[q : q + 1, :] - TOP_LOGW
        tail = jnp.concatenate([yr[128:192, at].astype(F32), bias_rows(bias, 0, 1.0), zeros56], 0)
        yt[at, 128:256] = jnp.transpose(tail).astype(BF16)
    arrive(there, c_recv.at[0])
    gsend[...] = combine([csend[...], crecv[...]])
    for n, z in enumerate(Z_PEERS):
        to_s((z, 0), me_z, gsend.at[0:13], grecv.at[me_z, 0:13], g_send.at[n], g_recv)
    grecv[me_z] = gsend[...]

    orders = (2, 1, 3, 0)
    for n, order in enumerate(orders):
        columns = pl.ds(pl.multiple_of(lax.rem(me_y + order, 4) * 256, 256), 256)
        for base, stop in ((0, 512), (512, 1024), (1024, 1664)):
            weights = jnp.exp2(dot(yt[base:stop, :], xr[:, columns]))
            high = weights.astype(BF16)
            wh[n, base:stop, :] = high
            wl[n, base:stop, :] = (weights - high.astype(F32)).astype(BF16)

    row = lall[pl.ds(me_y * 2 + me_x // 2, 1), :]
    row = jnp.where(lax.rem(me_t, 2) == 1, pltpu.roll(row, 64, 1), row)
    out_ref[32:33, :] = src_sq - (EPSILON / LOG2E) * row

    for z in reversed(Z_PEERS):
        slot = lax.rem(me_z + z, 8)
        arrive(grecv.at[slot, 0:13], g_recv.at[slot])
    col_lse = combine([grecv[k] for k in range(8)])
    gall[...] = col_lse
    factor = jnp.exp2(csend[...] - col_lse)
    for q in range(13):
        at = slice(128 * q, 128 * q + 128)
        scale = factor[q : q + 1, :]
        whole = tf[:, at] * scale
        one = whole.astype(BF16)
        scale_one = scale.astype(BF16).astype(F32)
        sub = sub_iota(16)
        line = jnp.where(sub == 0, scale_one, jnp.where(sub == 1, scale - scale_one, 0.0))
        tl[0:32, at] = one
        tl[32:48, at] = line.astype(BF16)
        tl[48:80, at] = (whole - one.astype(F32)).astype(BF16)
    def gather_moments(n):
        tile = lax.rem(me_y + orders[n], 4)
        main = dot(tl[...], wh[n])
        rest = dot(tl[0:48, :], wl[n])
        coords = main[0:32] + main[48:80] + rest[0:32]
        norms = main[32:40] + rest[32:40]
        norms = norms + pltpu.roll(norms, 7, 0)
        for u in range(4):
            lanes = slice(128 * (u // 2), 128 * (u // 2) + 128)
            one, two, three = coords[0:16, lanes], coords[16:32, lanes], norms[:, lanes]
            if u % 2 == 0:
                two = pltpu.roll(two, 64, 1)
            else:
                one, three = pltpu.roll(one, 64, 1), pltpu.roll(three, 64, 1)
            msend[tile * 4 + u, 0:16, :] = jnp.where(low, one, two)
            msend[tile * 4 + u, 16:24, :] = three

    for group in ((0, 1, 2), (3,)):
        for n in group:
            gather_moments(n)
        for n in group:
            order = orders[n]
            tile = lax.rem(me_y + order, 4)
            for x in range(0 if order else 1, 4):
                slot = tile * 4 + lax.rem(me_x + x, 4)
                to_t((order, x), msend.at[slot, 0:SRC_LINES], mrecv.at[me_t, 0:SRC_LINES],
                     m_send.at[order * 4 + x], m_recv)
    mrecv[me_t] = msend[me_t]

    start = me_s * OWN_COLS
    line, offset = start // 128, lax.rem(start, 128)
    here = pltpu.roll(gall[pl.ds(line, 1), :], 128 - offset, 1)
    after = pltpu.roll(gall[pl.ds(line + 1, 1), :], 128 - offset, 1)
    col = jnp.where(lane_iota(1) < 128 - offset, here, after)
    out_ref[33:34, :] = tgt_sq - (EPSILON / LOG2E) * col
    out_ref[34:40, :] = jnp.zeros((6, 128), F32)

    for offset in reversed(TGT_PEERS):
        slot = at_t(offset)
        arrive(mrecv.at[slot, 0:SRC_LINES], m_recv.at[slot])
    acc, norm = mrecv[0, 0:16, :], mrecv[0, 16:17, :]
    for k in range(1, GROUP):
        acc = acc + mrecv[k, 0:16, :]
        norm = norm + mrecv[k, 16:17, :]
    ratio = acc / jnp.where(low[0:1], norm, pltpu.roll(norm, 64, 1))
    out_ref[0:16, :] = ratio
    out_ref[16:32, :] = pltpu.roll(ratio, 64, 1)
    for copy in sent:
        copy.wait_send()


def deliver(out_ref, f_ref, g_ref, p_ref):
    f_ref[...] = out_ref[32:33, 0:OWN_ROWS]
    g_ref[...] = out_ref[33:34, 0:OWN_COLS]
    p_ref[...] = out_ref[0:DIM, 0:OWN_ROWS]


def body(source, target, target_pot, source_logw, target_logw):
    vmem = pl.BlockSpec(memory_space=pltpu.VMEM)
    out = pl.pallas_call(
        kernel,
        out_shape=pltpu.VMEM((40, 128), F32),
        in_specs=[pl.BlockSpec(memory_space=pl.ANY)] * 5,
        out_specs=vmem,
        scratch_shapes=[
            pltpu.VMEM((DIM, OWN_ROWS), F32),
            pltpu.VMEM((DIM, OWN_COLS), F32),
            pltpu.VMEM((1, OWN_COLS), F32),
            pltpu.VMEM((1, OWN_ROWS), F32),
            pltpu.VMEM((1, OWN_COLS), F32),
            pltpu.VMEM((40, 128), F32),
            pltpu.VMEM((24, 128), F32),
            pltpu.VMEM((40, 128), F32),
            pltpu.VMEM((GROUP, 24, 128), F32),
            pltpu.VMEM((2, 8, 40, 128), F32),
            pltpu.VMEM((256, ROWS), BF16),
            pltpu.VMEM((256, COLS), BF16),
            pltpu.VMEM((ROWS, 256), BF16),
            pltpu.VMEM((COLS, 256), BF16),
            pltpu.VMEM((80, COLS), BF16),
            pltpu.VMEM((DIM, COLS), F32),
            pltpu.VMEM((4, COLS, 256), BF16),
            pltpu.VMEM((4, COLS, 256), BF16),
            pltpu.VMEM((8, 2 * OWN_COLS, 256), BF16),
            pltpu.VMEM((2, 2 * OWN_COLS, ROWS), F32),
            pltpu.VMEM((2, 1, ROWS), F32),
            pltpu.VMEM((2, ROWS, 256), F32),
            pltpu.VMEM((8, 128), F32),
            pltpu.VMEM((16, 128), F32),
            pltpu.VMEM((8, 8, 128), F32),
            pltpu.VMEM((8, 128), F32),
            pltpu.VMEM((GROUP, 8, 128), F32),
            pltpu.VMEM((4, 16, 128), F32),
            pltpu.VMEM((16, 128), F32),
            pltpu.VMEM((16, 128), F32),
            pltpu.VMEM((16, 128), F32),
            pltpu.VMEM((8, 16, 128), F32),
            pltpu.VMEM((GROUP, 24, 128), F32),
            pltpu.VMEM((GROUP, 24, 128), F32),
            pltpu.VMEM((8, 128), F32),
            pltpu.VMEM((16, 128), F32),
            pltpu.SemaphoreType.DMA((5,)),
        ]
        + [pltpu.SemaphoreType.DMA((GROUP,))] * 6
        + [pltpu.SemaphoreType.DMA((GROUP,))] * 4
        + [pltpu.SemaphoreType.DMA((1,))] * 2,
        compiler_params=pltpu.CompilerParams(
            collective_id=0, has_side_effects=True, vmem_limit_bytes=60 * 1024 * 1024
        ),
    )(
        source,
        target,
        target_pot.reshape(1, OWN_COLS),
        source_logw.reshape(1, OWN_ROWS),
        target_logw.reshape(1, OWN_COLS),
    )
    f_new, g_new, projection = pl.pallas_call(
        deliver,
        out_shape=(
            jax.ShapeDtypeStruct((1, OWN_ROWS), F32),
            jax.ShapeDtypeStruct((1, OWN_COLS), F32),
            jax.ShapeDtypeStruct((DIM, OWN_ROWS), F32),
        ),
        in_specs=[vmem],
        out_specs=(vmem,) * 3,
    )(pltpu.with_memory_space_constraint(out, pltpu.VMEM))
    return f_new.reshape(OWN_ROWS), g_new.reshape(OWN_COLS), projection


def solution(mesh):
    return jax.shard_map(
        body,
        mesh=mesh,
        in_specs=(
            P(None, ("src", "tgt")),
            P(None, ("tgt", "src")),
            P(("tgt", "src")),
            P(("src", "tgt")),
            P(("tgt", "src")),
        ),
        out_specs=(P(("src", "tgt")), P(("tgt", "src")), P(None, ("src", "tgt"))),
        check_vma=False,
    )
```

```python
import math

import jax
import jax.numpy as jnp
from jax import lax
from jax.experimental import pallas as pl
from jax.experimental.pallas import tpu as pltpu
from jax.sharding import PartitionSpec as P

EPSILON = 0.05
LOG2E = 1.0 / math.log(2.0)
SCALE = LOG2E / EPSILON
TOP_LOGW = -9.0 * LOG2E
F32 = jnp.float32
BF16 = jnp.bfloat16
MESH = pl.DeviceIdType.MESH
GROUP = 16
ROWS = 1024
COLS = 1664
OWN_ROWS = 64
OWN_COLS = 104
DIM = 32
SRC_LINES = 17
TGT_LINES = 34


def ring(d, n):
    return min(d, n - d)


TGT_PEERS = sorted(
    [(y, x) for y in range(4) for x in range(4) if y or x],
    key=lambda o: -(ring(o[0], 4) + ring(o[1], 4)),
)
Z_PEERS = (4, 3, 5, 2, 6, 1, 7)


def dot(a, b):
    return lax.dot_general(a, b, (((1,), (0,)), ((), ())), preferred_element_type=F32)


def split3(x):
    one = x.astype(BF16).astype(F32)
    rest = x - one
    two = rest.astype(BF16).astype(F32)
    return one, two, rest - two


def lane_iota(rows):
    return lax.broadcasted_iota(jnp.int32, (rows, 128), 1)


def sub_iota(rows):
    return lax.broadcasted_iota(jnp.int32, (rows, 128), 0)


def bias_rows(bias, at=0, other=0.0):
    one, two, three = split3(bias)
    sub = sub_iota(8)
    rest = jnp.where(sub < 6, other, 0.0)
    return jnp.where(sub == at, one, jnp.where(sub == at + 1, two, jnp.where(sub == at + 2, three, rest)))


def combine(parts):
    top = parts[0]
    for part in parts[1:]:
        top = jnp.maximum(top, part)
    total = jnp.exp2(parts[0] - top)
    for part in parts[1:]:
        total = total + jnp.exp2(part - top)
    return top + jnp.log(total) * LOG2E


def column_pieces(block):
    start, pieces = block * 128, []
    while start < block * 128 + 128:
        shard, offset = divmod(start, OWN_COLS)
        stop = min((shard + 1) * OWN_COLS, block * 128 + 128)
        pieces.append((shard, offset, start - block * 128, stop - block * 128))
        start = stop
    return pieces


def lse(scores):
    top = jnp.max(scores, 0, keepdims=True)
    return top + jnp.log(jnp.sum(jnp.exp2(scores - top), 0, keepdims=True)) * LOG2E


def kernel(
    src_hbm, tgt_hbm, pot_hbm, slw_hbm, tlw_hbm,
    out_ref,
    src_v, tgt_v, pot_v, slw_v, tlw_v,
    pad, smsg, tmsg, srecv, trecv,
    xr, yr, xt, yt, tl, tf, cross, wh, wl, ya, held, peak, scr,
    slw, tlw, lpart, lsend, lrecv, cpart, csend, crecv, gsend, grecv, msend, mrecv, lall, gall,
    in_sem, s_send, s_recv, t_send, t_recv, l_send, l_recv, g_send, g_recv, m_send, m_recv, c_send, c_recv,
):
    me_t = lax.axis_index("tgt")
    me_s = lax.axis_index("src")
    me_y, me_x = me_t // 4, lax.rem(me_t, 4)
    me_z, me_c = me_s // 2, lax.rem(me_s, 2)

    def at_t(offset):
        return lax.rem(me_y + offset[0], 4) * 4 + lax.rem(me_x + offset[1], 4)

    def at_s(offset):
        return lax.rem(me_z + offset[0], 8) * 2 + lax.rem(me_c + offset[1], 2)

    barrier = pltpu.get_barrier_semaphore()
    for offset in [(z, 0) for z in Z_PEERS] + [(0, 1)]:
        pl.semaphore_signal(barrier, inc=1, device_id={"src": at_s(offset)}, device_id_type=MESH)
    for offset in TGT_PEERS:
        pl.semaphore_signal(barrier, inc=1, device_id={"tgt": at_t(offset)}, device_id_type=MESH)

    inputs = [
        pltpu.make_async_copy(a, b, in_sem.at[n])
        for n, (a, b) in enumerate(
            ((src_hbm, src_v), (slw_hbm, slw_v), (tgt_hbm, tgt_v), (pot_hbm, pot_v), (tlw_hbm, tlw_v))
        )
    ]
    for copy in inputs:
        copy.start()
    pad[...] = jnp.zeros_like(pad)
    tmsg[...] = jnp.zeros_like(tmsg)
    low = lane_iota(16) < 64
    for copy in inputs:
        copy.wait()

    pad[0:DIM, 0:OWN_ROWS] = src_v[...]
    pad[DIM : DIM + 1, 0:OWN_ROWS] = slw_v[...] * LOG2E
    own = pad[...]
    src_sq = jnp.sum(own[0:DIM] * own[0:DIM], 0, keepdims=True)
    smsg[0:16, :] = jnp.where(low, own[0:16], pltpu.roll(own[16:32], 64, 1))
    smsg[16:24, :] = own[32:40]
    tmsg[0:DIM, 0:OWN_COLS] = tgt_v[...]
    own_t = tmsg[0:DIM, :]
    tgt_sq = jnp.sum(own_t * own_t, 0, keepdims=True)
    tmsg[DIM : DIM + 1, 0:OWN_COLS] = (
        SCALE * (pot_v[...] - tgt_sq[:, 0:OWN_COLS]) + LOG2E * tlw_v[...]
    )
    tmsg[DIM + 1 : DIM + 2, 0:OWN_COLS] = LOG2E * tlw_v[...]

    pl.semaphore_wait(barrier, len(TGT_PEERS) + len(Z_PEERS) + 1)
    sent = []

    def to_t(offset, src, dst, send, recv):
        copy = pltpu.make_async_remote_copy(
            src_ref=src, dst_ref=dst, send_sem=send, recv_sem=recv.at[me_t],
            device_id={"tgt": at_t(offset)}, device_id_type=MESH,
        )
        copy.start()
        sent.append(copy)

    def to_s(offset, slot, src, dst, send, recv):
        copy = pltpu.make_async_remote_copy(
            src_ref=src, dst_ref=dst, send_sem=send, recv_sem=recv.at[slot],
            device_id={"src": at_s(offset)}, device_id_type=MESH,
        )
        copy.start()
        sent.append(copy)

    def arrive(dst, sem):
        pltpu.make_async_copy(dst, dst, sem).wait()

    tgt_own = tmsg.at[0:TGT_LINES]
    for n, z in enumerate(Z_PEERS):
        to_s((z, 0), 8 - z, tgt_own, trecv.at[0, 8 - z, 0:TGT_LINES], t_send.at[n], t_recv)
    src_own = smsg.at[0:SRC_LINES]
    for n, offset in enumerate(TGT_PEERS):
        to_t(offset, src_own, srecv.at[me_t, 0:SRC_LINES], s_send.at[n], s_recv)
    srecv[me_t] = smsg[...]
    trecv[0, 0] = tmsg[...]
    ones16 = jnp.where(sub_iota(16) < 3, 1.0, 0.0).astype(BF16)
    zeros48 = jnp.zeros((48, 128), BF16)
    zeros56 = jnp.zeros((56, 128), F32)

    def operand(n):
        tops_t, tails_t = [], []
        for z in (2 * n, 2 * n + 1):
            block = trecv[z // 8, z % 8]
            y1, y2, y3 = split3(block[0:DIM])
            tops_t.append(jnp.transpose(jnp.concatenate([y1, y2, y1, y2], 0))[0:OWN_COLS])
            tail = jnp.concatenate([y3, y1, bias_rows(block[DIM : DIM + 1]), zeros56], 0)
            tails_t.append(jnp.transpose(tail)[0:OWN_COLS])
        ya[n, :, 0:128] = jnp.concatenate(tops_t, 0).astype(BF16)
        ya[n, :, 128:256] = jnp.concatenate(tails_t, 0).astype(BF16)

    def second(n):
        for t in range(4):
            part = lse(dot(ya[n], xr[:, 256 * t : 256 * t + 256]))
            lpart[n, 2 * t : 2 * t + 1, :] = part[:, 0:128]
            lpart[n, 2 * t + 1 : 2 * t + 2, :] = part[:, 128:256]

    for z in reversed(Z_PEERS):
        arrive(trecv.at[0, 8 - z, 0:TGT_LINES], t_recv.at[8 - z])
    to_s((0, 1), 8, trecv.at[0, :, 0:TGT_LINES], trecv.at[1, :, 0:TGT_LINES], t_send.at[7], t_recv)
    operand(0)

    for offset in reversed(TGT_PEERS):
        slot = at_t(offset)
        arrive(srecv.at[slot, 0:SRC_LINES], s_recv.at[slot])
    for p in range(8):
        a, b = srecv[2 * p], srecv[2 * p + 1]
        one = jnp.where(low, a[0:16], pltpu.roll(b[0:16], 64, 1))
        two = jnp.where(low, pltpu.roll(a[0:16], 64, 1), b[0:16])
        x1, x2, x3 = split3(jnp.concatenate([one, two], 0) * (2.0 * SCALE))
        at = slice(128 * p, 128 * p + 128)
        slw[p : p + 1, :] = jnp.where(low[0:1], a[16:17], pltpu.roll(b[16:24], 64, 1)[0:1])
        xr[0:128, at] = jnp.concatenate([x1, x1, x2, x2], 0).astype(BF16)
        xr[128:192, at] = jnp.concatenate([x1, x3], 0).astype(BF16)
        xr[192:208, at] = ones16
        xr[208:256, at] = zeros48
    second(0)
    for n in range(1, 4):
        operand(n)
        second(n)
    arrive(trecv.at[1, :, 0:TGT_LINES], t_recv.at[8])
    for n in range(4, 8):
        operand(n)
        second(n)
    lsend[...] = combine([lpart[n] for n in range(8)])
    for n, offset in enumerate(TGT_PEERS):
        to_t(offset, lsend, lrecv.at[me_t], l_send.at[n], l_recv)
    lrecv[me_t] = lsend[...]

    for p in range(8):
        at = slice(128 * p, 128 * p + 128)
        xt[at, 0:128] = jnp.transpose(xr[0:128, at].astype(F32)).astype(BF16)
    for q in range(13):
        at = slice(128 * q, 128 * q + 128)
        lane = lane_iota(40)
        block = None
        for shard, offset, start, stop in column_pieces(q):
            piece = trecv[lax.rem(shard + me_c, 2), lax.rem(shard // 2 + 8 - me_z, 8)]
            shift = (start - offset) % 128
            if shift:
                piece = pltpu.roll(piece, shift, 1)
            block = piece if block is None else jnp.where(lane >= start, piece, block)
        y1, y2, y3 = split3(block[0:DIM])
        tlw[q : q + 1, :] = block[DIM + 1 : DIM + 2]
        yr[0:128, at] = jnp.concatenate([y1, y2, y1, y2], 0).astype(BF16)
        yr[128:192, at] = jnp.concatenate([y3, y1], 0).astype(BF16)
        yr[192:208, at] = ones16
        yr[208:256, at] = zeros48
        yt[at, 0:128] = jnp.transpose(jnp.concatenate([y1, y2, y1, y2], 0)).astype(BF16)
        tf[:, at] = block[0:DIM]

    for p in range(8):
        at = slice(128 * p, 128 * p + 128)
        tail = jnp.concatenate([xr[128:192, at].astype(F32), jnp.zeros((64, 128), F32)], 0)
        xt[at, 128:256] = jnp.transpose(tail).astype(BF16)
    for r in range(4):
        rows = slice(256 * r, 256 * r + 256)
        for n in range(7):
            columns = slice(256 * n, min(256 * n + 256, COLS))
            cross[rows, columns] = dot(xt[rows, :], yr[:, columns])

    for offset in reversed(TGT_PEERS):
        slot = at_t(offset)
        arrive(lrecv.at[slot], l_recv.at[slot])
    row_lse = combine([lrecv[k] for k in range(GROUP)])
    lall[...] = row_lse
    bias = slw[...] - row_lse

    for r in range(8):
        tall = jnp.transpose(jnp.broadcast_to(bias[r : r + 1, :], (128, 128)))
        for n in range(7):
            width = min(256, COLS - 256 * n)
            columns = slice(256 * n, 256 * n + width)
            here = cross[128 * r : 128 * r + 128, columns] + jnp.concatenate([tall] * (width // 128), 1)
            here = here.reshape(16, 8, width)
            top = jnp.max(here, 0)
            cpart[r, :, columns] = top + jnp.log(jnp.sum(jnp.exp2(here - top), 0)) * LOG2E
    for q in range(13):
        columns = slice(128 * q, 128 * q + 128)
        csend[q : q + 1, :] = lse(cpart[:, :, columns].reshape(64, 128))
    there = crecv.at[0:13]
    copy = pltpu.make_async_remote_copy(
        src_ref=csend.at[0:13], dst_ref=there, send_sem=c_send.at[0], recv_sem=c_recv.at[0],
        device_id={"src": at_s((0, 1))}, device_id_type=MESH,
    )
    copy.start()
    sent.append(copy)
    for p in range(8):
        at = slice(128 * p, 128 * p + 128)
        both = jnp.concatenate([bias_rows(bias[p : p + 1, :], 3, 1.0), jnp.zeros((8, 128), F32)], 0)
        xr[192:208, at] = both.astype(BF16)
    for q in range(13):
        at = slice(128 * q, 128 * q + 128)
        bias = tlw[q : q + 1, :] - csend[q : q + 1, :] - TOP_LOGW
        tail = jnp.concatenate([yr[128:192, at].astype(F32), bias_rows(bias, 0, 1.0), zeros56], 0)
        yt[at, 128:256] = jnp.transpose(tail).astype(BF16)
    arrive(there, c_recv.at[0])
    gsend[...] = combine([csend[...], crecv[...]])
    for n, z in enumerate(Z_PEERS):
        to_s((z, 0), me_z, gsend.at[0:13], grecv.at[me_z, 0:13], g_send.at[n], g_recv)
    grecv[me_z] = gsend[...]

    orders = (2, 1, 3, 0)
    for n, order in enumerate(orders):
        columns = pl.ds(pl.multiple_of(lax.rem(me_y + order, 4) * 256, 256), 256)
        for base, stop in ((0, 512), (512, 1024), (1024, 1664)):
            weights = jnp.exp2(dot(yt[base:stop, :], xr[:, columns]))
            high = weights.astype(BF16)
            wh[n, base:stop, :] = high
            wl[n, base:stop, :] = (weights - high.astype(F32)).astype(BF16)

    row = lall[pl.ds(me_y * 2 + me_x // 2, 1), :]
    row = jnp.where(lax.rem(me_t, 2) == 1, pltpu.roll(row, 64, 1), row)
    out_ref[32:33, :] = src_sq - (EPSILON / LOG2E) * row

    for z in reversed(Z_PEERS):
        slot = lax.rem(me_z + z, 8)
        arrive(grecv.at[slot, 0:13], g_recv.at[slot])
    col_lse = combine([grecv[k] for k in range(8)])
    gall[...] = col_lse
    factor = jnp.exp2(csend[...] - col_lse)
    for q in range(13):
        at = slice(128 * q, 128 * q + 128)
        scale = factor[q : q + 1, :]
        whole = tf[:, at] * scale
        one = whole.astype(BF16)
        scale_one = scale.astype(BF16).astype(F32)
        sub = sub_iota(16)
        line = jnp.where(sub == 0, scale_one, jnp.where(sub == 1, scale - scale_one, 0.0))
        tl[0:32, at] = one
        tl[32:48, at] = line.astype(BF16)
        tl[48:80, at] = (whole - one.astype(F32)).astype(BF16)
    def gather_moments(n):
        tile = lax.rem(me_y + orders[n], 4)
        main = dot(tl[...], wh[n])
        rest = dot(tl[0:48, :], wl[n])
        coords = main[0:32] + main[48:80] + rest[0:32]
        norms = main[32:40] + rest[32:40]
        norms = norms + pltpu.roll(norms, 7, 0)
        for u in range(4):
            lanes = slice(128 * (u // 2), 128 * (u // 2) + 128)
            one, two, three = coords[0:16, lanes], coords[16:32, lanes], norms[:, lanes]
            if u % 2 == 0:
                two = pltpu.roll(two, 64, 1)
            else:
                one, three = pltpu.roll(one, 64, 1), pltpu.roll(three, 64, 1)
            msend[tile * 4 + u, 0:16, :] = jnp.where(low, one, two)
            msend[tile * 4 + u, 16:24, :] = three

    for group in ((0, 1), (2, 3)):
        for n in group:
            gather_moments(n)
        for n in group:
            order = orders[n]
            tile = lax.rem(me_y + order, 4)
            for x in range(0 if order else 1, 4):
                slot = tile * 4 + lax.rem(me_x + x, 4)
                to_t((order, x), msend.at[slot, 0:SRC_LINES], mrecv.at[me_t, 0:SRC_LINES],
                     m_send.at[order * 4 + x], m_recv)
    mrecv[me_t] = msend[me_t]

    start = me_s * OWN_COLS
    line, offset = start // 128, lax.rem(start, 128)
    here = pltpu.roll(gall[pl.ds(line, 1), :], 128 - offset, 1)
    after = pltpu.roll(gall[pl.ds(line + 1, 1), :], 128 - offset, 1)
    col = jnp.where(lane_iota(1) < 128 - offset, here, after)
    out_ref[33:34, :] = tgt_sq - (EPSILON / LOG2E) * col
    out_ref[34:40, :] = jnp.zeros((6, 128), F32)

    for offset in reversed(TGT_PEERS):
        slot = at_t(offset)
        arrive(mrecv.at[slot, 0:SRC_LINES], m_recv.at[slot])
    acc, norm = mrecv[0, 0:16, :], mrecv[0, 16:17, :]
    for k in range(1, GROUP):
        acc = acc + mrecv[k, 0:16, :]
        norm = norm + mrecv[k, 16:17, :]
    ratio = acc / jnp.where(low[0:1], norm, pltpu.roll(norm, 64, 1))
    out_ref[0:16, :] = ratio
    out_ref[16:32, :] = pltpu.roll(ratio, 64, 1)
    for copy in sent:
        copy.wait_send()


def deliver(out_ref, f_ref, g_ref, p_ref):
    f_ref[...] = out_ref[32:33, 0:OWN_ROWS]
    g_ref[...] = out_ref[33:34, 0:OWN_COLS]
    p_ref[...] = out_ref[0:DIM, 0:OWN_ROWS]


def body(source, target, target_pot, source_logw, target_logw):
    vmem = pl.BlockSpec(memory_space=pltpu.VMEM)
    out = pl.pallas_call(
        kernel,
        out_shape=pltpu.VMEM((40, 128), F32),
        in_specs=[pl.BlockSpec(memory_space=pl.ANY)] * 5,
        out_specs=vmem,
        scratch_shapes=[
            pltpu.VMEM((DIM, OWN_ROWS), F32),
            pltpu.VMEM((DIM, OWN_COLS), F32),
            pltpu.VMEM((1, OWN_COLS), F32),
            pltpu.VMEM((1, OWN_ROWS), F32),
            pltpu.VMEM((1, OWN_COLS), F32),
            pltpu.VMEM((40, 128), F32),
            pltpu.VMEM((24, 128), F32),
            pltpu.VMEM((40, 128), F32),
            pltpu.VMEM((GROUP, 24, 128), F32),
            pltpu.VMEM((2, 8, 40, 128), F32),
            pltpu.VMEM((256, ROWS), BF16),
            pltpu.VMEM((256, COLS), BF16),
            pltpu.VMEM((ROWS, 256), BF16),
            pltpu.VMEM((COLS, 256), BF16),
            pltpu.VMEM((80, COLS), BF16),
            pltpu.VMEM((DIM, COLS), F32),
            pltpu.VMEM((ROWS, COLS), F32),
            pltpu.VMEM((4, COLS, 256), BF16),
            pltpu.VMEM((4, COLS, 256), BF16),
            pltpu.VMEM((8, 2 * OWN_COLS, 256), BF16),
            pltpu.VMEM((2, 2 * OWN_COLS, ROWS), F32),
            pltpu.VMEM((2, 1, ROWS), F32),
            pltpu.VMEM((2, ROWS, 256), F32),
            pltpu.VMEM((8, 128), F32),
            pltpu.VMEM((16, 128), F32),
            pltpu.VMEM((8, 8, 128), F32),
            pltpu.VMEM((8, 128), F32),
            pltpu.VMEM((GROUP, 8, 128), F32),
            pltpu.VMEM((8, 8, COLS), F32),
            pltpu.VMEM((16, 128), F32),
            pltpu.VMEM((16, 128), F32),
            pltpu.VMEM((16, 128), F32),
            pltpu.VMEM((8, 16, 128), F32),
            pltpu.VMEM((GROUP, 24, 128), F32),
            pltpu.VMEM((GROUP, 24, 128), F32),
            pltpu.VMEM((8, 128), F32),
            pltpu.VMEM((16, 128), F32),
            pltpu.SemaphoreType.DMA((5,)),
        ]
        + [pltpu.SemaphoreType.DMA((GROUP,))] * 6
        + [pltpu.SemaphoreType.DMA((GROUP,))] * 4
        + [pltpu.SemaphoreType.DMA((1,))] * 2,
        compiler_params=pltpu.CompilerParams(
            collective_id=0, has_side_effects=True, vmem_limit_bytes=60 * 1024 * 1024
        ),
    )(
        source,
        target,
        target_pot.reshape(1, OWN_COLS),
        source_logw.reshape(1, OWN_ROWS),
        target_logw.reshape(1, OWN_COLS),
    )
    f_new, g_new, projection = pl.pallas_call(
        deliver,
        out_shape=(
            jax.ShapeDtypeStruct((1, OWN_ROWS), F32),
            jax.ShapeDtypeStruct((1, OWN_COLS), F32),
            jax.ShapeDtypeStruct((DIM, OWN_ROWS), F32),
        ),
        in_specs=[vmem],
        out_specs=(vmem,) * 3,
    )(pltpu.with_memory_space_constraint(out, pltpu.VMEM))
    return f_new.reshape(OWN_ROWS), g_new.reshape(OWN_COLS), projection


def solution(mesh):
    return jax.shard_map(
        body,
        mesh=mesh,
        in_specs=(
            P(None, ("src", "tgt")),
            P(None, ("tgt", "src")),
            P(("tgt", "src")),
            P(("src", "tgt")),
            P(("tgt", "src")),
        ),
        out_specs=(P(("src", "tgt")), P(("tgt", "src")), P(None, ("src", "tgt"))),
        check_vma=False,
    )
```
